128 devices in a mesh: ctx: 16 (over y, x), head: 8 (over z, core).
Axes of the slice: x: 4, y: 4, z: 4, core: 2. Of those that a mesh axis runs over, the one named last changes fastest.
Arguments:
- queries: bfloat16 [2048, 8192], P('ctx', 'head'), may hold values from -6 to 6
- keys_in: bfloat16 [2048, 1024], P('ctx', 'head'), may hold values from -6 to 6
- values_in: bfloat16 [2048, 1024], P('ctx', 'head'), may hold values from -6 to 6
- attn_cotan: bfloat16 [2048, 8192], P('ctx', 'head'), may hold values from -6 to 6
- doc_ids: int32 [2048], P('ctx'), may hold values from 0 to 5, never falling along the last dimension, each value on 1 to 1024 neighbouring positions
- ssd_input: bfloat16 [2048, 16384], P('ctx', 'head'), may hold values from -0.29882812 to 0.29882812
- state_write: bfloat16 [2048, 256], P('ctx'), may hold values from -0.375 to 0.375
- state_read: bfloat16 [2048, 256], P('ctx'), may hold values from -6 to 6
- log_decay: float32 [2048, 256], P('ctx', 'head'), may hold values from -1.3 to 0
- ssd_cotan: bfloat16 [2048, 16384], P('ctx', 'head'), may hold values from -0.119628906 to 0.119628906
Outputs:
- attn_out: bfloat16 [2048, 8192], P('ctx', 'head')
- ssd_out: bfloat16 [2048, 16384], P('ctx', 'head')
- grad_q: bfloat16 [2048, 8192], P('ctx', 'head')
- grad_k: bfloat16 [2048, 1024], P('ctx', 'head')
- grad_v: bfloat16 [2048, 1024], P('ctx', 'head')
- grad_x: bfloat16 [2048, 16384], P('ctx', 'head')
- grad_b: bfloat16 [2048, 256], P(('ctx', 'head'))
- grad_c: bfloat16 [2048, 256], P(('ctx', 'head'))
The draws below stay inside these ranges and needn't reach their ends.
Inputs may be any that keep to these rules, and one draw needn't show every extreme that they name: doc_ids never fall along the sequence; each document has 1 to 1024 tokens and one has exactly that many.
All inputs are finite; a program needn't handle non-finite values.
Results may differ from the reference program's by a relative error of at most 0.035.
Values may be sent and summed in bfloat16 or wider, within the bound.
A program may use at most 128 MiB of HBM per device.

```python
import math
import jax
import jax.numpy as jnp
import numpy as np
from jax import lax

QH = 64
KVH = 8
HD = 128
SPACE_HEADS = 256
P_SIZE = 64
N = 256
TOK_DEV = 128
PACKED_TOKENS = 2048


def drawn_pair(key):
    base = jax.random.fold_in(key, 7301)
    query_seed, key_seed = jax.random.split(base, 2)
    query_cols = QH * HD
    key_cols = KVH * HD
    query_raw = jnp.clip(jax.random.normal(query_seed, (PACKED_TOKENS, query_cols), jnp.float32), -4.0, 4.0)
    key_raw = jnp.clip(jax.random.normal(key_seed, (PACKED_TOKENS, key_cols), jnp.float32), -4.0, 4.0)
    return (query_raw, key_raw)


def draw_queries(key, part):
    return drawn_pair(key)[0].astype(jnp.bfloat16)


def draw_keys_in(key, part):
    return drawn_pair(key)[1].astype(jnp.bfloat16)


def draw_log_decay(key, part):
    base = jax.random.fold_in(key, 4409)
    random_seeds = jax.random.split(base, 7)
    fast_share = 0.5
    fast_heads = jax.random.uniform(random_seeds[0], (SPACE_HEADS,), jnp.float32) < fast_share
    fast_rate = jnp.exp(jax.random.uniform(random_seeds[1], (SPACE_HEADS,), jnp.float32, math.log(1.0 / 50.0), math.log(1.0 / 30.0)))
    slow_rate = jnp.exp(jax.random.uniform(random_seeds[2], (SPACE_HEADS,), jnp.float32, math.log(0.15), math.log(0.45))) / PACKED_TOKENS
    arrival_rate = jnp.where(fast_heads, fast_rate, slow_rate)
    device_multiplier = jnp.exp(jax.random.uniform(random_seeds[3], (PACKED_TOKENS // TOK_DEV, SPACE_HEADS), jnp.float32, math.log(0.7), math.log(1.4)))
    device_multiplier = jnp.repeat(device_multiplier, TOK_DEV, axis=0)
    token_multiplier = jax.random.uniform(random_seeds[4], (PACKED_TOKENS, SPACE_HEADS), jnp.float32, 0.7, 1.4)
    spurt_rows = jax.random.randint(random_seeds[5], (2, SPACE_HEADS), 1, PACKED_TOKENS)
    spurt_length = jnp.exp(jax.random.uniform(random_seeds[6], (2, SPACE_HEADS), jnp.float32, math.log(0.22), math.log(0.6)))
    matched_flag = (jnp.arange(PACKED_TOKENS)[:, None, None] == spurt_rows[None, :, :]).astype(jnp.float32)
    spurt_count = jnp.sum(matched_flag * spurt_length[None, :, :], axis=1)
    return -(arrival_rate[None, :] * device_multiplier * token_multiplier) - spurt_count


def steps_of(rng, extent, shards, least, top_value):
    def one(axis_at, parts):
        steps = jax.random.uniform(jax.random.fold_in(jax.random.fold_in(rng, 6), axis_at), (parts,), jnp.float32, least / len(shards), top_value / len(shards))
        return jnp.repeat(jnp.exp(steps), extent[axis_at] // parts).reshape((-1,) + (1,) * (len(extent) - axis_at - 1))

    gain = one(*shards[0])
    for cut in shards[1:]:
        gain = gain * one(*cut)
    return gain


def split_up(count, total, limit, lean):
    loads = [(1 << 20) // math.isqrt(rank ** lean) + 1 for rank in range(2, count + 1)]
    surplus, counts = total - limit - (count - 1), [1] * (count - 1)
    while surplus > 0:
        movable = [i for i in range(count - 1) if counts[i] < limit]
        whole, remaining = sum([loads[i] for i in movable]), surplus
        for i in movable:
            more = min(limit - counts[i], max(1, remaining * loads[i] // whole), surplus)
            counts[i] = counts[i] + more
            surplus = surplus - more
    return np.array([limit] + counts)


def ragged_sizes(rng, count, total, most, lean):
    if count == 2:
        one = jax.random.randint(rng, (), max(1, total - most), min(most, total - 1) + 1)
        return jnp.stack([one, total - one])
    lengths = jnp.asarray(split_up(count, total, most, lean), jnp.int32)
    couples = (count - 1) // 2
    source_of, sink = lengths[1:1 + 2 * couples:2], lengths[2:2 + 2 * couples:2]
    room = jnp.minimum(source_of - 1, most - sink)
    passed = jax.random.randint(jax.random.fold_in(rng, 1), (couples,), 0, 1 << 20) % (room + 1)
    lengths = lengths.at[1:1 + 2 * couples:2].set(source_of - passed).at[2:2 + 2 * couples:2].set(sink + passed)
    return lengths[jax.random.permutation(jax.random.fold_in(rng, 2), count)]


def noise(stream_key, extent, scale, most, cuts=(), kind=jnp.bfloat16):
    values = jax.random.normal(stream_key, extent, jnp.float32) * scale
    if len(cuts) > 0:
        values = steps_of(stream_key, extent, cuts, -0.22, 0.18) * values
    return jnp.clip(values, min=-most, max=most).astype(kind)


def setup_inputs(seed: int = 0) -> dict:
    splits = jax.random.split(jax.random.key(seed), 11)
    queries = draw_queries(jax.random.fold_in(splits[10], 71), 0)
    keys_in = draw_keys_in(jax.random.fold_in(splits[10], 71), 0)
    values_in = noise(splits[2], (PACKED_TOKENS, KVH * HD), 1.0, 6.0, ((0, 16), (1, 8)))
    attn_cotan = noise(splits[3], (PACKED_TOKENS, QH * HD), 1.0, 6.0, ((0, 16), (1, 8)))
    doc_ids = jnp.searchsorted(jnp.cumsum(ragged_sizes(splits[4], 6, PACKED_TOKENS, PACKED_TOKENS // 2, 0)), jnp.arange(PACKED_TOKENS), side="right").astype(jnp.int32)
    ssd_input = noise(splits[5], (PACKED_TOKENS, SPACE_HEADS * P_SIZE), 0.05, 0.29882812, ((0, 16), (1, 8)))
    state_write = noise(splits[6], (PACKED_TOKENS, N), N ** -0.5, 0.375, ((0, 16),))
    state_read = noise(splits[7], (PACKED_TOKENS, N), 1.0, 6.0, ((0, 16),))
    log_decay = draw_log_decay(jax.random.fold_in(splits[10], 71), 0)
    ssd_cotan = noise(splits[9], (PACKED_TOKENS, SPACE_HEADS * P_SIZE), 0.02, 0.119628906, ((0, 16), (1, 8)))
    return {"queries": queries, "keys_in": keys_in, "values_in": values_in, "attn_cotan": attn_cotan, "doc_ids": doc_ids, "ssd_input": ssd_input, "state_write": state_write, "state_read": state_read, "log_decay": log_decay, "ssd_cotan": ssd_cotan}


floor_score = -1.0e30
highest = lax.Precision.HIGHEST


def attention_part(queries, keys_in, values_in, attn_cotan, doc_ids):
    length = doc_ids.shape[0]
    group_size = QH // KVH
    scale = HD ** -0.5
    positions = jnp.arange(length, dtype=jnp.int32)
    allowed = (positions[None, :] <= positions[:, None]) & (doc_ids[None, :] == doc_ids[:, None])

    def one_head(head_index):
        kv_index = head_index // group_size
        query_head = lax.dynamic_slice_in_dim(queries, head_index * HD, HD, 1)
        key_head = lax.dynamic_slice_in_dim(keys_in, kv_index * HD, HD, 1)
        value_head = lax.dynamic_slice_in_dim(values_in, kv_index * HD, HD, 1)
        cotan_head = lax.dynamic_slice_in_dim(attn_cotan, head_index * HD, HD, 1)
        scores = jnp.dot(query_head, key_head.T, preferred_element_type=jnp.float32) * scale
        row_top = jnp.max(jnp.where(allowed, scores, floor_score), axis=1)
        weights = jnp.where(allowed, jnp.exp(scores - row_top[:, None]), 0.0)
        row_total = jnp.sum(weights, axis=1)
        attn_head = (jnp.dot(weights.astype(jnp.bfloat16), value_head, preferred_element_type=jnp.float32) / row_total[:, None]).astype(jnp.bfloat16)
        log_total = row_top + jnp.log(row_total)
        row_inner = jnp.sum(cotan_head.astype(jnp.float32) * attn_head.astype(jnp.float32), axis=1)
        attn_prob = jnp.where(allowed, jnp.exp(scores - log_total[:, None]), 0.0)
        prob_grad = jnp.dot(cotan_head, value_head.T, preferred_element_type=jnp.float32)
        dscore = (attn_prob * (prob_grad - row_inner[:, None])).astype(jnp.bfloat16)
        grad_query = (jnp.dot(dscore, key_head, preferred_element_type=jnp.float32) * scale).astype(jnp.bfloat16)
        grad_key = jnp.dot(dscore.T, query_head, preferred_element_type=jnp.float32) * scale
        grad_value = jnp.dot(attn_prob.astype(jnp.bfloat16).T, cotan_head, preferred_element_type=jnp.float32)
        return attn_head, grad_query, grad_key, grad_value

    heads_out, grads_q, grads_k, grads_v = lax.map(one_head, jnp.arange(QH, dtype=jnp.int32))
    attn_out = heads_out.transpose(1, 0, 2).reshape(length, QH * HD)
    grad_q = grads_q.transpose(1, 0, 2).reshape(length, QH * HD)
    grad_k = grads_k.reshape(KVH, group_size, length, HD).sum(axis=1).astype(jnp.bfloat16)
    grad_k = grad_k.transpose(1, 0, 2).reshape(length, KVH * HD)
    grad_v = grads_v.reshape(KVH, group_size, length, HD).sum(axis=1).astype(jnp.bfloat16)
    grad_v = grad_v.transpose(1, 0, 2).reshape(length, KVH * HD)
    return attn_out, grad_q, grad_k, grad_v


def ssd_part(ssd_input, state_write, state_read, log_decay, ssd_cotan, doc_ids):
    length = doc_ids.shape[0]
    input_wide = ssd_input.astype(jnp.float32).reshape(length, SPACE_HEADS, P_SIZE)
    cotan_wide = ssd_cotan.astype(jnp.float32).reshape(length, SPACE_HEADS, P_SIZE)
    write_wide = state_write.astype(jnp.float32)
    read_wide = state_read.astype(jnp.float32)
    same_doc = jnp.concatenate([jnp.zeros((1,), dtype=bool), doc_ids[1:] == doc_ids[:-1]])
    factor = jnp.where(same_doc[:, None], jnp.exp(log_decay), 0.0)

    def forward(carried, step_inputs):
        step_factor, input_row, write_row, read_row, cotan_row = step_inputs
        carried = step_factor[:, None, None] * carried + input_row[:, :, None] * write_row[None, None, :]
        output_row = jnp.einsum("hpn,n->hp", carried, read_row, precision=highest)
        read_grad = jnp.einsum("hpn,hp->n", carried, cotan_row, precision=highest)
        return carried, (output_row, read_grad)

    empty_state = jnp.zeros((SPACE_HEADS, P_SIZE, N), jnp.float32)
    _, (outputs, grad_c) = lax.scan(forward, empty_state, (factor, input_wide, write_wide, read_wide, cotan_wide))
    next_factor = jnp.concatenate([factor[1:], jnp.zeros((1, SPACE_HEADS), jnp.float32)], axis=0)

    def backward(carried, step_inputs):
        step_factor, input_row, write_row, read_row, cotan_row = step_inputs
        carried = step_factor[:, None, None] * carried + cotan_row[:, :, None] * read_row[None, None, :]
        input_grad = jnp.einsum("hpn,n->hp", carried, write_row, precision=highest)
        write_grad = jnp.einsum("hpn,hp->n", carried, input_row, precision=highest)
        return carried, (input_grad, write_grad)

    _, (grad_x, grad_b) = lax.scan(backward, empty_state, (next_factor, input_wide, write_wide, read_wide, cotan_wide), reverse=True)
    ssd_out = outputs.reshape(length, SPACE_HEADS * P_SIZE).astype(jnp.bfloat16)
    grad_x = grad_x.reshape(length, SPACE_HEADS * P_SIZE).astype(jnp.bfloat16)
    return ssd_out, grad_x, grad_b.astype(jnp.bfloat16), grad_c.astype(jnp.bfloat16)


def reference(queries, keys_in, values_in, attn_cotan, doc_ids, ssd_input, state_write, state_read, log_decay, ssd_cotan):
    attn_out, grad_q, grad_k, grad_v = attention_part(queries, keys_in, values_in, attn_cotan, doc_ids)
    ssd_out, grad_x, grad_b, grad_c = ssd_part(ssd_input, state_write, state_read, log_decay, ssd_cotan, doc_ids)
    return (attn_out, ssd_out, grad_q, grad_k, grad_v, grad_x, grad_b, grad_c)
```

```python
import jax
import jax.numpy as jnp
from jax import lax
from jax.experimental import pallas as pl
from jax.experimental.pallas import tpu as pltpu
from jax.sharding import PartitionSpec as P

MESH = pl.DeviceIdType.MESH
F32 = jnp.float32
BF16 = jnp.bfloat16
NEG = -1.0e30
SCALE = 128.0**-0.5

T = 128
CTX = 16
NX = 4
HEADS = 8
QL = 8
WIN = 9
KEYS = WIN * T
N = 256
GL = 512
NG = 4

NN = (((1,), (0,)), ((), ()))
NT = (((1,), (1,)), ((), ()))
TN = (((0,), (0,)), ((), ()))


def dot(a, b, dims=NN):
    return lax.dot_general(a, b, dims, preferred_element_type=F32)


def remote(src, dst, send, recv, device):
    return pltpu.make_async_remote_copy(
        src_ref=src,
        dst_ref=dst,
        send_sem=send,
        recv_sem=recv,
        device_id=device,
        device_id_type=MESH,
    )


def lanes(i, width):
    return pl.ds(pl.multiple_of(i * width, width), width)


def column_of(row):
    return jnp.broadcast_to(row, (T, T)).T


def kernel(
    q_ref,
    k_ref,
    v_ref,
    do_ref,
    doc_ref,
    x_ref,
    b_ref,
    c_ref,
    ld_ref,
    ct_ref,
    ao_ref,
    so_ref,
    gq_ref,
    gk_ref,
    gv_ref,
    gx_ref,
    gb_ref,
    gc_ref,
    kwin,
    vwin,
    kt,
    vt,
    docs,
    bias,
    qs,
    dos,
    pall,
    dsall,
    dkv_own,
    dkv_s,
    dkv_r,
    xg,
    cg,
    bg,
    rg,
    cumr,
    dg,
    ccol,
    lo,
    lgx,
    wsum,
    gbl,
    wst,
    wen,
    xe,
    cs,
    sst,
    gst,
    lst,
    rst,
    lout,
    bout_l,
    prow,
    drow,
    erow,
    cin,
    cout,
    bin_,
    bout,
    so_s,
    gx_s,
    gbc_s,
    so_r,
    gx_r,
    gbc_r,
    gsum,
    gr,
    doc_ss,
    doc_rs,
    xa_ss,
    xa_rs,
    kv_ss,
    kv_rs,
    cf_ss,
    cf_rs,
    cb_ss,
    cb_rs,
    out_ss,
    out_rs,
    dkv_ss,
    dkv_rs,
    z_ss,
    z_rs,
):
    c = lax.axis_index("ctx")
    h = lax.axis_index("head")
    y = c // NX
    x = lax.rem(c, NX)

    def ctx_at(d):
        return (lax.rem(c + d + CTX, CTX), h)

    def row_at(d):
        return y * NX + lax.rem(x + d, NX)

    barrier = pltpu.get_barrier_semaphore()

    def greet_ctx(d, carry):
        pl.semaphore_signal(barrier, inc=1, device_id=ctx_at(d), device_id_type=MESH)
        return carry

    def greet_head(d, carry):
        pl.semaphore_signal(
            barrier, inc=1, device_id=(c, lax.rem(h + d, HEADS)), device_id_type=MESH
        )
        return carry

    lax.fori_loop(1, CTX, greet_ctx, 0)
    lax.fori_loop(1, HEADS, greet_head, 0)

    row_i = lax.broadcasted_iota(jnp.int32, (T, T), 0)
    col_i = lax.broadcasted_iota(jnp.int32, (T, T), 1)
    upto = (row_i <= col_i).astype(F32)
    low_half = col_i < 64

    decay_t = jnp.concatenate([ld_ref[...], jnp.zeros((T, T - 32), F32)], axis=1).T
    cumr[...] = lax.dot_general(
        decay_t[:32], upto, NN, precision=lax.Precision.HIGHEST, preferred_element_type=F32
    )

    pl.semaphore_wait(barrier, CTX - 1 + HEADS - 1)

    def doc_copy(d):
        return remote(doc_ref, docs.at[c], doc_ss.at[d], doc_rs.at[d], ctx_at(d))

    def doc_send(d, carry):
        doc_copy(d).start()
        return carry

    lax.fori_loop(1, CTX, doc_send, 0)

    def group_copies(d):
        t = lax.rem(x + d, NX)
        device = (y * NX + t, h)
        pairs = (
            (cumr.at[pl.ds(pl.multiple_of(t * 8, 8), 8)], dg.at[x]),
            (b_ref, bg.at[x]),
            (x_ref.at[:, lanes(t, GL)], xg.at[x]),
            (c_ref, rg.at[x]),
            (ct_ref.at[:, lanes(t, GL)], cg.at[x]),
        )
        return [
            remote(src, dst, xa_ss.at[d * 5 + i], xa_rs.at[d * 5 + i], device)
            for i, (src, dst) in enumerate(pairs)
        ]

    sends = {d: group_copies(d) for d in (1, 2, 3)}
    for i in range(5):
        for d in (1, 3, 2):
            sends[d][i].start()

    def kv_copies(o):
        rows = pl.ds(pl.multiple_of(o * T, T), T)
        return (
            remote(k_ref, kwin.at[rows], kv_ss.at[2 * o], kv_rs.at[2 * o], ctx_at(o)),
            remote(v_ref, vwin.at[rows], kv_ss.at[2 * o + 1], kv_rs.at[2 * o + 1], ctx_at(o)),
        )

    def kv_send(o, carry):
        for copy in kv_copies(o):
            copy.start()
        return carry

    lax.fori_loop(1, WIN, kv_send, 0)

    kwin[0:T, :] = k_ref[...]
    vwin[0:T, :] = v_ref[...]
    docs[c] = doc_ref[...]
    xg[x] = x_ref[:, lanes(x, GL)]
    cg[x] = ct_ref[:, lanes(x, GL)]
    bg[x] = b_ref[...]
    rg[x] = c_ref[...]
    dg[x] = cumr[pl.ds(pl.multiple_of(x * 8, 8), 8), :]

    doc_row = doc_ref[...].astype(F32)
    doc_col = column_of(doc_row)
    local_bias = jnp.where((doc_row == doc_col) & (col_i <= row_i), 0.0, NEG)
    gram = dot(c_ref[...], b_ref[...], NT)
    wsum[...] = jnp.zeros((T, T), F32)

    def columns(g, carry):
        rows = cumr[pl.ds(pl.multiple_of(g * 8, 8), 8), :]
        ccol[g] = jnp.concatenate([rows, jnp.zeros((T - 8, T), F32)], axis=0).T
        return carry

    lax.fori_loop(0, NG, columns, 0)
    half_mask = low_half.astype(BF16)
    other_mask = (~low_half).astype(BF16)

    def local_group(g, carry):
        rows = cumr[pl.ds(pl.multiple_of(g * 8, 8), 8), :]
        cols = ccol[g]
        total = wsum[...]
        for p in range(4):
            at = lanes(g * 4 + p, T)
            xp = x_ref[:, at]
            cp = ct_ref[:, at]
            x2 = jnp.concatenate([xp * half_mask, xp * other_mask], axis=0)
            c2 = jnp.concatenate([cp * half_mask, cp * other_mask], axis=0)
            inner = dot(c2, xp, NT)
            mix = []
            for i in range(2):
                j = 2 * p + i
                decay = jnp.exp(cols[:, j : j + 1] - rows[j : j + 1, :] + local_bias)
                mix.append((decay * gram).astype(BF16))
                total = total + decay * inner[i * T : (i + 1) * T]
            lo[:, at] = dot(jnp.concatenate(mix, axis=1), x2)
            lgx[:, at] = dot(jnp.concatenate(mix, axis=0), c2, TN)
        wsum[...] = total
        return carry

    lax.fori_loop(0, NG, local_group, 0)
    weighted = wsum[...].astype(BF16)
    gbl[:, 0:N] = dot(weighted, c_ref[...], TN)
    gbl[:, N : 2 * N] = dot(weighted, b_ref[...])

    def doc_wait(d, carry):
        doc_copy(d).wait_recv()
        return carry

    lax.fori_loop(1, CTX, doc_wait, 0)
    for i in range(5):
        for d in (1, 3, 2):
            sends[d][i].wait_recv()

    lane_half = lax.broadcasted_iota(jnp.int32, (T, T), 1) < 64

    def block_sums(j, carry):
        cum = dg[j]
        docj = docs[y * NX + j].astype(F32)
        start = jnp.where(docj == docj[:, 0:1], 1.0, 0.0)
        end = jnp.where(docj == docj[:, T - 1 : T], 1.0, 0.0)
        w_start = jnp.exp(cum) * start
        w_end = jnp.exp(cum[:, T - 1 : T] - cum) * end
        table = jnp.concatenate([w_start, w_end, jnp.zeros((T - 16, T), F32)], axis=0).T
        for p in range(4):
            at = slice(p * T, (p + 1) * T)
            ws = jnp.where(lane_half, table[:, 2 * p : 2 * p + 1], table[:, 2 * p + 1 : 2 * p + 2])
            we = jnp.where(
                lane_half, table[:, 8 + 2 * p : 9 + 2 * p], table[:, 9 + 2 * p : 10 + 2 * p]
            )
            wst[j, :, at] = ws
            wen[j, :, at] = we
            prow[j, :, at] = ws[T - 1 : T, :]
            xe[j, :, at] = (xg[j, :, at].astype(F32) * we).astype(BF16)
            cs[j, :, at] = (cg[j, :, at].astype(F32) * ws).astype(BF16)
        sst[j] = dot(bg[j], xe[j], TN)
        gst[j] = dot(rg[j], cs[j], TN)
        return carry

    lax.fori_loop(0, NX, block_sums, 0)

    def edge(j, side):
        at = 0 if side == 0 else T - 1
        return docs[j].astype(F32)[:, at : at + 1]

    def linked(first, last, inside):
        same = edge(first, 0) == edge(last, 1)
        return jnp.where(same & inside, 1.0, 0.0)

    base = y * NX
    link = [linked(base, jnp.maximum(base - 1, 0), y > 0)]
    link += [linked(base + j, base + j - 1, y >= 0) for j in range(1, NX)]
    link += [linked(jnp.minimum(base + NX, CTX - 1), base + NX - 1, y < NX - 1)]
    wide = [jnp.broadcast_to(value, (1, GL)) for value in link]

    drow[0] = wide[0]
    lst[0] = jnp.zeros((N, GL), F32)
    for j in range(NX - 1):
        lst[j + 1] = wide[j + 1] * (prow[j] * lst[j] + sst[j])
        drow[j + 1] = wide[j + 1] * prow[j] * drow[j]
    lout[...] = prow[NX - 1] * lst[NX - 1] + sst[NX - 1]
    drow[NX] = prow[NX - 1] * drow[NX - 1]
    erow[NX - 1] = wide[NX]
    rst[NX - 1] = jnp.zeros((N, GL), F32)
    for j in range(NX - 1, 0, -1):
        rst[j - 1] = wide[j] * (prow[j] * rst[j] + gst[j])
        erow[j - 1] = wide[j] * prow[j] * erow[j]
    bout_l[...] = prow[0] * rst[0] + gst[0]
    erow[NX] = prow[0] * erow[0]

    @pl.when(y == 0)
    def _():
        cin[...] = jnp.zeros((N, GL), BF16)

    @pl.when(y == NX - 1)
    def _():
        bin_[...] = jnp.zeros((N, GL), BF16)

    def forward_copy(p):
        device = (lax.rem(c + NX, CTX), h)
        return remote(cout.at[p], cin.at[:, lanes(p, T)], cf_ss.at[p], cf_rs.at[p], device)

    def backward_copy(p):
        device = (lax.rem(c + CTX - NX, CTX), h)
        return remote(bout.at[p], bin_.at[:, lanes(p, T)], cb_ss.at[p], cb_rs.at[p], device)

    def forward_step(p):
        at = lanes(p, T)

        @pl.when(y > 0)
        def _():
            forward_copy(p).wait_recv()

        @pl.when(y < NX - 1)
        def _():
            value = lout[:, at] + drow[NX, :, at] * cin[:, at].astype(F32)
            cout[p] = value.astype(BF16)
            forward_copy(p).start()

    def backward_step(p):
        at = lanes(p, T)

        @pl.when(y < NX - 1)
        def _():
            backward_copy(p).wait_recv()

        @pl.when(y > 0)
        def _():
            value = bout_l[:, at] + erow[NX, :, at] * bin_[:, at].astype(F32)
            bout[p] = value.astype(BF16)
            backward_copy(p).start()

    def kv_wait(o, carry):
        for copy in kv_copies(o):
            copy.wait_recv()
        return carry

    def window_block(o, carry):
        rows = pl.ds(pl.multiple_of(o * T, T), T)
        kb = lax.rem(c - o + CTX, CTX)
        key_doc = column_of(docs[kb].astype(F32))
        allowed = (key_doc == doc_row) & (kb * T + row_i <= c * T + col_i)
        bias[rows, :] = jnp.where(allowed, 0.0, NEG)
        kt[:, rows] = kwin[rows, :].T
        vt[:, rows] = vwin[rows, :].T
        return carry

    def head_step(i):
        at = lanes(i, T)
        rows = pl.ds(pl.multiple_of(i * T, T), T)
        qh = q_ref[:, at]
        doh = do_ref[:, at]
        qs[rows, :] = qh
        dos[rows, :] = doh
        scores = dot(kwin[...], qh, NT) * SCALE + bias[...]
        top = jnp.max(scores, axis=0, keepdims=True)
        weights = jnp.exp(scores - top)
        total = jnp.sum(weights, axis=0, keepdims=True)
        out_t = dot(vt[...], weights.astype(BF16)) / total
        ao_ref[:, at] = out_t.T.astype(BF16)
        low = out_t.astype(BF16).astype(F32)
        inner = jnp.sum(low * doh.astype(F32).T, axis=0, keepdims=True)
        prob = weights * (1.0 / total)
        dscore = (prob * (dot(vwin[...], doh, NT) - inner)).astype(BF16)
        pall[:, at] = prob.astype(BF16)
        dsall[:, at] = dscore
        gq_ref[:, at] = (dot(kt[...], dscore) * SCALE).T.astype(BF16)

    def mixed(step, carry):
        pf = step - 2 * y
        pb = step - 2 * (NX - 1 - y)

        @pl.when((pf >= 0) & (pf < 4))
        def _():
            forward_step(pf)

        @pl.when((pb >= 0) & (pb < 4))
        def _():
            backward_step(pb)

        @pl.when(step == 0)
        def _():
            lax.fori_loop(1, WIN, kv_wait, 0)
            lax.fori_loop(0, WIN, window_block, 0)

        @pl.when(step < QL)
        def _():
            head_step(step)

        return carry

    lax.fori_loop(0, 2 * (NX - 1) + 4, mixed, 0)

    def grads_copy(o):
        return remote(dkv_s.at[o], dkv_r.at[o], dkv_ss.at[o], dkv_rs.at[o], ctx_at(-o))

    def grads_block(o, carry):
        rows = pl.ds(pl.multiple_of(o * T, T), T)
        dkv_s[o, :, 0:T] = (dot(dsall[rows, :], qs[...]) * SCALE).astype(BF16)
        dkv_s[o, :, T : 2 * T] = dot(pall[rows, :], dos[...]).astype(BF16)
        grads_copy(o).start()
        return carry

    def out_copies(d):
        j = lax.rem(x + d, NX)
        device = (y * NX + j, h)
        pairs = ((so_s.at[j], so_r.at[x]), (gx_s.at[j], gx_r.at[x]), (gbc_s.at[j], gbc_r.at[x]))
        return [
            remote(src, dst, out_ss.at[d * 3 + i], out_rs.at[d * 3 + i], device)
            for i, (src, dst) in enumerate(pairs)
        ]

    def inter(j):
        state = (lst[j] + drow[j] * cin[...].astype(F32)).astype(BF16)
        back = (rst[j] + erow[j] * bin_[...].astype(F32)).astype(BF16)
        out = (dot(rg[j], state) * wst[j]).astype(BF16)
        gx = (dot(bg[j], back) * wen[j]).astype(BF16)
        gb = dot(xe[j], back, NT).astype(BF16)
        gc = dot(cs[j], state, NT).astype(BF16)
        return out, gx, gb, gc

    def inter_send(d, carry):
        j = lax.rem(x + d, NX)
        out, gx, gb, gc = inter(j)
        so_s[j] = out
        gx_s[j] = gx
        gbc_s[j, :, 0:N] = gb
        gbc_s[j, :, N : 2 * N] = gc
        for copy in out_copies(d):
            copy.start()
        return carry

    lax.fori_loop(1, NX, inter_send, 0)
    out, gx, gb, gc = inter(x)
    so_r[x] = out
    gx_r[x] = gx
    gbc_r[x, :, 0:N] = gb
    gbc_r[x, :, N : 2 * N] = gc

    lax.fori_loop(1, WIN, grads_block, 0)
    own = slice(0, T)
    dkv_own[:, 0:T] = dot(dsall[own, :], qs[...]) * SCALE
    dkv_own[:, T : 2 * T] = dot(pall[own, :], dos[...])

    for d in (1, 2, 3):
        for copy in out_copies(d):
            copy.wait_recv()

    for s in range(NX):
        at = slice(s * GL, (s + 1) * GL)
        so_ref[:, at] = (lo[:, at] + so_r[s].astype(F32)).astype(BF16)
        gx_ref[:, at] = (lgx[:, at] + gx_r[s].astype(F32)).astype(BF16)

    shared = gbl[...]
    for s in range(NX):
        shared = shared + gbc_r[s].astype(F32)
    for e in range(HEADS):
        gsum[e] = shared[e * 16 : (e + 1) * 16, :].astype(BF16)

    def head_copy(d):
        e = lax.rem(h + d, HEADS)
        return remote(gsum.at[e], gr.at[h], z_ss.at[d], z_rs.at[d], (c, e))

    def head_send(d, carry):
        head_copy(d).start()
        return carry

    lax.fori_loop(1, HEADS, head_send, 0)
    gr[h] = gsum[h]

    def grads_wait(o, carry):
        grads_copy(o).wait_recv()
        dkv_own[...] += dkv_r[o].astype(F32)
        return carry

    lax.fori_loop(1, WIN, grads_wait, 0)
    gk_ref[...] = dkv_own[:, 0:T].astype(BF16)
    gv_ref[...] = dkv_own[:, T : 2 * T].astype(BF16)

    def head_wait(d, carry):
        head_copy(d).wait_recv()
        return carry

    lax.fori_loop(1, HEADS, head_wait, 0)
    merged = gr[0].astype(F32)
    for e in range(1, HEADS):
        merged = merged + gr[e].astype(F32)
    gb_ref[...] = merged[:, 0:N].astype(BF16)
    gc_ref[...] = merged[:, N : 2 * N].astype(BF16)

    def doc_done(d, carry):
        doc_copy(d).wait_send()
        return carry

    def kv_done(o, carry):
        for copy in kv_copies(o):
            copy.wait_send()
        grads_copy(o).wait_send()
        return carry

    def head_done(d, carry):
        head_copy(d).wait_send()
        return carry

    def chain_done(p, carry):
        @pl.when(y < NX - 1)
        def _():
            forward_copy(p).wait_send()

        @pl.when(y > 0)
        def _():
            backward_copy(p).wait_send()

        return carry

    lax.fori_loop(1, CTX, doc_done, 0)
    lax.fori_loop(1, WIN, kv_done, 0)
    lax.fori_loop(0, 4, chain_done, 0)
    for d in (1, 2, 3):
        for copy in sends[d] + out_copies(d):
            copy.wait_send()
    lax.fori_loop(1, HEADS, head_done, 0)


def body(q, k, v, do, doc, xs, b, cr, ld, ct):
    vm = pltpu.VMEM
    dma = pltpu.SemaphoreType.DMA
    scratch = [
        vm((KEYS, T), BF16),
        vm((KEYS, T), BF16),
        vm((T, KEYS), BF16),
        vm((T, KEYS), BF16),
        vm((CTX, 1, T), jnp.int32),
        vm((KEYS, T), F32),
        vm((QL * T, T), BF16),
        vm((QL * T, T), BF16),
        vm((KEYS, QL * T), BF16),
        vm((KEYS, QL * T), BF16),
        vm((T, 2 * T), F32),
        vm((WIN, T, 2 * T), BF16),
        vm((WIN, T, 2 * T), BF16),
        vm((NX, T, GL), BF16),
        vm((NX, T, GL), BF16),
        vm((NX, T, N), BF16),
        vm((NX, T, N), BF16),
        vm((32, T), F32),
        vm((NX, 8, T), F32),
        vm((NG, T, T), F32),
        vm((T, NG * GL), F32),
        vm((T, NG * GL), F32),
        vm((T, T), F32),
        vm((T, 2 * N), F32),
        vm((NX, T, GL), F32),
        vm((NX, T, GL), F32),
        vm((NX, T, GL), BF16),
        vm((NX, T, GL), BF16),
        vm((NX, N, GL), F32),
        vm((NX, N, GL), F32),
        vm((NX, N, GL), F32),
        vm((NX, N, GL), F32),
        vm((N, GL), F32),
        vm((N, GL), F32),
        vm((NX, 1, GL), F32),
        vm((NX + 1, 1, GL), F32),
        vm((NX + 1, 1, GL), F32),
        vm((N, GL), BF16),
        vm((4, N, T), BF16),
        vm((N, GL), BF16),
        vm((4, N, T), BF16),
        vm((NX, T, GL), BF16),
        vm((NX, T, GL), BF16),
        vm((NX, T, 2 * N), BF16),
        vm((NX, T, GL), BF16),
        vm((NX, T, GL), BF16),
        vm((NX, T, 2 * N), BF16),
        vm((HEADS, 16, 2 * N), BF16),
        vm((HEADS, 16, 2 * N), BF16),
        dma((CTX,)),
        dma((CTX,)),
        dma((20,)),
        dma((20,)),
        dma((2 * WIN,)),
        dma((2 * WIN,)),
        dma((4,)),
        dma((4,)),
        dma((4,)),
        dma((4,)),
        dma((12,)),
        dma((12,)),
        dma((WIN,)),
        dma((WIN,)),
        dma((HEADS,)),
        dma((HEADS,)),
    ]
    shape = jax.ShapeDtypeStruct
    return pl.pallas_call(
        kernel,
        name="packed_layers",
        out_shape=(
            shape((T, QL * T), BF16),
            shape((T, NG * GL), BF16),
            shape((T, QL * T), BF16),
            shape((T, T), BF16),
            shape((T, T), BF16),
            shape((T, NG * GL), BF16),
            shape((T // HEADS, N), BF16),
            shape((T // HEADS, N), BF16),
        ),
        in_specs=[pl.BlockSpec(memory_space=pltpu.VMEM)] * 10,
        out_specs=[pl.BlockSpec(memory_space=pltpu.VMEM)] * 8,
        scratch_shapes=scratch,
        compiler_params=pltpu.CompilerParams(
            collective_id=0, has_side_effects=True, vmem_limit_bytes=60 * 1024 * 1024
        ),
    )(q, k, v, do, doc.reshape(1, T), xs, b, cr, ld, ct)


def solution(mesh):
    both = P("ctx", "head")
    tokens = P("ctx", None)
    shared = P(("ctx", "head"), None)
    return jax.shard_map(
        body,
        mesh=mesh,
        in_specs=(both, both, both, both, P("ctx"), both, tokens, tokens, both, both),
        out_specs=(both, both, both, both, both, both, shared, shared),
        check_vma=False,
    )
```

```python
import jax
import jax.numpy as jnp
from jax import lax
from jax.experimental import pallas as pl
from jax.experimental.pallas import tpu as pltpu
from jax.sharding import PartitionSpec as P

MESH = pl.DeviceIdType.MESH
F32 = jnp.float32
BF16 = jnp.bfloat16
NEG = -1.0e30
SCALE = 128.0**-0.5

T = 128
CTX = 16
NX = 4
HEADS = 8
QL = 8
WIN = 9
KEYS = WIN * T
N = 256
GL = 512
NG = 4

NN = (((1,), (0,)), ((), ()))
NT = (((1,), (1,)), ((), ()))
TN = (((0,), (0,)), ((), ()))


def dot(a, b, dims=NN):
    return lax.dot_general(a, b, dims, preferred_element_type=F32)


def remote(src, dst, send, recv, device):
    return pltpu.make_async_remote_copy(
        src_ref=src,
        dst_ref=dst,
        send_sem=send,
        recv_sem=recv,
        device_id=device,
        device_id_type=MESH,
    )


def lanes(i, width):
    return pl.ds(pl.multiple_of(i * width, width), width)


def column_of(row):
    return jnp.broadcast_to(row, (T, T)).T


def kernel(
    q_hbm,
    k_hbm,
    v_hbm,
    do_hbm,
    doc_ref,
    x_hbm,
    b_hbm,
    c_hbm,
    ld_ref,
    ct_hbm,
    ao_ref,
    so_ref,
    gq_ref,
    gk_ref,
    gv_ref,
    gx_ref,
    gb_ref,
    gc_ref,
    q_ref,
    do_ref,
    x_ref,
    b_ref,
    c_ref,
    ct_ref,
    kwin,
    vwin,
    kt,
    vt,
    docs,
    bias,
    qs,
    dos,
    pall,
    dsall,
    dkv_own,
    dkv_s,
    dkv_r,
    xg,
    cg,
    bg,
    rg,
    cumr,
    dg,
    ccol,
    lo,
    lgx,
    wsum,
    gbl,
    wst,
    wen,
    xe,
    cs,
    sst,
    gst,
    lst,
    rst,
    lout,
    bout_l,
    prow,
    drow,
    erow,
    cin,
    cout,
    bin_,
    bout,
    so_s,
    gx_s,
    so_r,
    gx_r,
    gb_acc,
    gc_acc,
    gb_s,
    gc_s,
    gb_r,
    gc_r,
    gsum,
    gr,
    in_sem,
    doc_ss,
    doc_rs,
    xa_ss,
    xa_rs,
    kv_ss,
    kv_rs,
    cf_ss,
    cf_rs,
    cb_ss,
    cb_rs,
    bc_ss,
    bc_rs,
    hd_ss,
    hd_rs,
    of_ss,
    of_rs,
    ob_ss,
    ob_rs,
    gg_ss,
    gg_rs,
    dkv_ss,
    dkv_rs,
    z_ss,
    z_rs,
):
    c = lax.axis_index("ctx")
    h = lax.axis_index("head")
    y = c // NX
    x = lax.rem(c, NX)

    def ctx_at(d):
        return (lax.rem(c + d + CTX, CTX), h)

    def row_at(d):
        return y * NX + lax.rem(x + d, NX)

    barrier = pltpu.get_barrier_semaphore()

    def greet_ctx(d, carry):
        pl.semaphore_signal(barrier, inc=1, device_id=ctx_at(d), device_id_type=MESH)
        return carry

    def greet_head(d, carry):
        pl.semaphore_signal(
            barrier, inc=1, device_id=(c, lax.rem(h + d, HEADS)), device_id_type=MESH
        )
        return carry

    lax.fori_loop(1, CTX, greet_ctx, 0)
    lax.fori_loop(1, HEADS, greet_head, 0)

    own_rows = pl.ds(0, T)
    loads = [
        pltpu.make_async_copy(src, dst, in_sem.at[i])
        for i, (src, dst) in enumerate(
            (
                (b_hbm, b_ref),
                (c_hbm, c_ref),
                (x_hbm, x_ref),
                (ct_hbm, ct_ref),
                (k_hbm, kwin.at[own_rows]),
                (v_hbm, vwin.at[own_rows]),
                (q_hbm, q_ref),
                (do_hbm, do_ref),
            )
        )
    ]
    for load in loads:
        load.start()

    row_i = lax.broadcasted_iota(jnp.int32, (T, T), 0)
    col_i = lax.broadcasted_iota(jnp.int32, (T, T), 1)
    upto = (row_i <= col_i).astype(F32)
    low_half = col_i < 64

    cumr[...] = lax.dot_general(
        ld_ref[...], upto, NN, precision=lax.Precision.HIGHEST, preferred_element_type=F32
    )
    my_slab = pl.ds(pl.multiple_of(h * 16, 16), 16)

    pl.semaphore_wait(barrier, CTX - 1 + HEADS - 1)

    def doc_copy(d):
        return remote(doc_ref, docs.at[c], doc_ss.at[d], doc_rs.at[d], ctx_at(d))

    def doc_send(d, carry):
        doc_copy(d).start()
        return carry

    def slab_copies(d):
        device = (row_at(d), h)
        pairs = ((b_hbm, bg), (c_hbm, rg))
        return [
            remote(
                src.at[my_slab],
                dst.at[x, my_slab],
                bc_ss.at[d * 2 + i],
                bc_rs.at[d * 2 + i],
                device,
            )
            for i, (src, dst) in enumerate(pairs)
        ]

    def share_copies(d):
        device = (c, lax.rem(h + d, HEADS))
        return [
            remote(
                ref.at[:, my_slab, :],
                ref.at[:, my_slab, :],
                hd_ss.at[d * 2 + i],
                hd_rs.at[d * 2 + i],
                device,
            )
            for i, ref in enumerate((bg, rg))
        ]

    def group_copies(d):
        t = lax.rem(x + d, NX)
        device = (y * NX + t, h)
        pairs = (
            (cumr.at[pl.ds(pl.multiple_of(t * 8, 8), 8)], dg.at[x]),
            (x_hbm.at[:, lanes(t, GL)], xg.at[x]),
            (ct_hbm.at[:, lanes(t, GL)], cg.at[x]),
        )
        return [
            remote(src, dst, xa_ss.at[d * 3 + i], xa_rs.at[d * 3 + i], device)
            for i, (src, dst) in enumerate(pairs)
        ]

    slabs = {d: slab_copies(d) for d in (1, 3, 2)}
    sends = {d: group_copies(d) for d in (1, 3, 2)}
    for d in (1, 3, 2):
        for copy in slabs[d]:
            copy.start()
        sends[d][0].start()
    lax.fori_loop(1, CTX, doc_send, 0)

    def kv_copies(o):
        rows = pl.ds(pl.multiple_of(o * T, T), T)
        return (
            remote(k_hbm, kwin.at[rows], kv_ss.at[2 * o], kv_rs.at[2 * o], ctx_at(o)),
            remote(v_hbm, vwin.at[rows], kv_ss.at[2 * o + 1], kv_rs.at[2 * o + 1], ctx_at(o)),
        )

    def kv_send(o, carry):
        @pl.when(c + o < CTX)
        def _():
            for copy in kv_copies(o):
                copy.start()

        @pl.when(c < o)
        def _():
            rows = pl.ds(pl.multiple_of(o * T, T), T)
            kwin[rows, :] = jnp.zeros((T, T), BF16)
            vwin[rows, :] = jnp.zeros((T, T), BF16)

        return carry

    kv_send(NX, 0)
    kv_send(2 * NX, 0)
    for i in (1, 2):
        for d in (1, 3, 2):
            sends[d][i].start()
    lax.fori_loop(1, NX, kv_send, 0)
    lax.fori_loop(NX + 1, 2 * NX, kv_send, 0)

    for load in loads:
        load.wait()
    docs[c] = doc_ref[...]
    xg[x] = x_ref[:, lanes(x, GL)]
    cg[x] = ct_ref[:, lanes(x, GL)]
    bg[x, my_slab, :] = b_ref[my_slab, :]
    rg[x, my_slab, :] = c_ref[my_slab, :]
    dg[x] = cumr[pl.ds(pl.multiple_of(x * 8, 8), 8), :]

    doc_row = doc_ref[...].astype(F32)
    doc_col = column_of(doc_row)
    local_bias = jnp.where((doc_row == doc_col) & (col_i <= row_i), 0.0, NEG)
    gram = dot(c_ref[...], b_ref[...], NT)
    wsum[...] = jnp.zeros((T, T), F32)

    def columns(g, carry):
        rows = cumr[pl.ds(pl.multiple_of(g * 8, 8), 8), :]
        ccol[g] = jnp.concatenate([rows, jnp.zeros((T - 8, T), F32)], axis=0).T
        return carry

    lax.fori_loop(0, NG, columns, 0)
    half_mask = low_half.astype(BF16)
    other_mask = (~low_half).astype(BF16)

    def local_group(g, carry):
        rows = cumr[pl.ds(pl.multiple_of(g * 8, 8), 8), :]
        cols = ccol[g]
        total = wsum[...]
        for p in range(4):
            at = lanes(g * 4 + p, T)
            xp = x_ref[:, at]
            cp = ct_ref[:, at]
            x2 = jnp.concatenate([xp * half_mask, xp * other_mask], axis=0)
            c2 = jnp.concatenate([cp * half_mask, cp * other_mask], axis=0)
            inner = dot(c2, xp, NT)
            mix = []
            for i in range(2):
                j = 2 * p + i
                decay = jnp.exp(cols[:, j : j + 1] - rows[j : j + 1, :] + local_bias)
                mix.append((decay * gram).astype(BF16))
                total = total + decay * inner[i * T : (i + 1) * T]
            lo[:, at] = dot(jnp.concatenate(mix, axis=1), x2)
            lgx[:, at] = dot(jnp.concatenate(mix, axis=0), c2, TN)
        wsum[...] = total
        return carry

    lax.fori_loop(0, NG, local_group, 0)
    weighted = wsum[...].astype(BF16)
    gbl[:, 0:N] = dot(weighted, c_ref[...], TN)
    gbl[:, N : 2 * N] = dot(weighted, b_ref[...])

    for d in (1, 3, 2):
        for copy in slabs[d]:
            copy.wait_recv()

    def share(d, carry):
        for copy in share_copies(d):
            copy.start()
        return carry

    lax.fori_loop(1, HEADS, share, 0)

    def doc_wait(d, carry):
        doc_copy(d).wait_recv()
        return carry

    lax.fori_loop(1, CTX, doc_wait, 0)
    for d in (1, 3, 2):
        sends[d][0].wait_recv()

    def weights_of(j, carry):
        cum = dg[j]
        docj = docs[y * NX + j].astype(F32)
        start = jnp.where(docj == docj[:, 0:1], 1.0, 0.0)
        end = jnp.where(docj == docj[:, T - 1 : T], 1.0, 0.0)
        w_start = jnp.exp(cum) * start
        w_end = jnp.exp(cum[:, T - 1 : T] - cum) * end
        table = jnp.concatenate([w_start, w_end, jnp.zeros((T - 16, T), F32)], axis=0).T
        for p in range(4):
            at = slice(p * T, (p + 1) * T)
            ws = jnp.where(low_half, table[:, 2 * p : 2 * p + 1], table[:, 2 * p + 1 : 2 * p + 2])
            we = jnp.where(
                low_half, table[:, 8 + 2 * p : 9 + 2 * p], table[:, 9 + 2 * p : 10 + 2 * p]
            )
            wst[j, :, at] = ws
            wen[j, :, at] = we
            prow[j, :, at] = ws[T - 1 : T, :]
        return carry

    lax.fori_loop(0, NX, weights_of, 0)

    def edge(j, side):
        at = 0 if side == 0 else T - 1
        return docs[j].astype(F32)[:, at : at + 1]

    def linked(first, last, inside):
        same = edge(first, 0) == edge(last, 1)
        return jnp.where(same & inside, 1.0, 0.0)

    base = y * NX
    link = [linked(base, jnp.maximum(base - 1, 0), y > 0)]
    link += [linked(base + j, base + j - 1, y >= 0) for j in range(1, NX)]
    link += [linked(jnp.minimum(base + NX, CTX - 1), base + NX - 1, y < NX - 1)]
    wide = [jnp.broadcast_to(value, (1, GL)) for value in link]

    drow[0] = wide[0]
    for j in range(NX - 1):
        drow[j + 1] = wide[j + 1] * prow[j] * drow[j]
    drow[NX] = prow[NX - 1] * drow[NX - 1]
    erow[NX - 1] = wide[NX]
    for j in range(NX - 1, 0, -1):
        erow[j - 1] = wide[j] * prow[j] * erow[j]
    erow[NX] = prow[0] * erow[0]

    @pl.when(y == 0)
    def _():
        cin[...] = jnp.zeros((N, GL), BF16)

    @pl.when(y == NX - 1)
    def _():
        bin_[...] = jnp.zeros((N, GL), BF16)

    def bias_block(o, carry):
        rows = pl.ds(pl.multiple_of(o * T, T), T)
        kb = lax.rem(c - o + CTX, CTX)
        key_doc = column_of(docs[kb].astype(F32))
        allowed = (key_doc == doc_row) & (kb * T + row_i <= c * T + col_i)
        block = jnp.where(allowed, 0.0, NEG)
        bias[rows, 0:T] = block
        bias[rows, T : 2 * T] = block
        return carry

    def stack_head(i, carry):
        rows = pl.ds(pl.multiple_of(i * T, T), T)
        qs[rows, :] = q_ref[:, lanes(i, T)]
        dos[rows, :] = do_ref[:, lanes(i, T)]
        return carry

    lax.fori_loop(0, WIN, bias_block, 0)
    lax.fori_loop(0, QL, stack_head, 0)

    for i in (1, 2):
        for d in (1, 3, 2):
            sends[d][i].wait_recv()

    def share_wait(d, carry):
        for copy in share_copies(d):
            copy.wait_recv()
        return carry

    lax.fori_loop(1, HEADS, share_wait, 0)

    def block_sums(j, carry):
        xe[j] = (xg[j].astype(F32) * wen[j]).astype(BF16)
        cs[j] = (cg[j].astype(F32) * wst[j]).astype(BF16)
        sst[j] = dot(bg[j], xe[j], TN)
        gst[j] = dot(rg[j], cs[j], TN)
        gc_acc[j] = jnp.zeros((T, N), F32)
        gb_acc[j] = jnp.zeros((T, N), F32)
        return carry

    lax.fori_loop(0, NX, block_sums, 0)
    lst[0] = jnp.zeros((N, GL), F32)
    for j in range(NX - 1):
        lst[j + 1] = wide[j + 1] * (prow[j] * lst[j] + sst[j])
    lout[...] = prow[NX - 1] * lst[NX - 1] + sst[NX - 1]
    rst[NX - 1] = jnp.zeros((N, GL), F32)
    for j in range(NX - 1, 0, -1):
        rst[j - 1] = wide[j] * (prow[j] * rst[j] + gst[j])
    bout_l[...] = prow[0] * rst[0] + gst[0]

    def forward_copy(p):
        device = (lax.rem(c + NX, CTX), h)
        return remote(cout.at[p], cin.at[:, lanes(p, T)], cf_ss.at[p], cf_rs.at[p], device)

    def backward_copy(p):
        device = (lax.rem(c + CTX - NX, CTX), h)
        return remote(bout.at[p], bin_.at[:, lanes(p, T)], cb_ss.at[p], cb_rs.at[p], device)

    def forward_send(p):
        at = lanes(p, T)
        value = lout[:, at] + drow[NX, :, at] * cin[:, at].astype(F32)
        cout[p] = value.astype(BF16)
        forward_copy(p).start()

    def backward_send(p):
        at = lanes(p, T)
        value = bout_l[:, at] + erow[NX, :, at] * bin_[:, at].astype(F32)
        bout[p] = value.astype(BF16)
        backward_copy(p).start()

    def piece_copy(p, d, mine, theirs, send, recv):
        j = lax.rem(x + d, NX)
        k = p * NX + d
        return remote(mine.at[p, j], theirs.at[p, x], send.at[k], recv.at[k], (y * NX + j, h))

    def shared_copy(d, mine, theirs, k):
        e = lax.rem(h + d, HEADS)
        k = 2 * d + k
        return remote(mine.at[e], theirs.at[h], z_ss.at[k], z_rs.at[k], (c, e))

    def piece(p, local, scale, carried, proj, weight, terms, acc, mine, theirs, send, recv):
        at = lanes(p, T)
        value = carried[:, at].astype(F32)
        for d in (1, 3, 2, 0):
            j = lax.rem(x + d, NX)
            state = (local[j, :, at] + scale[j, :, at] * value).astype(BF16)
            out = (dot(proj[j], state) * weight[j, :, at]).astype(BF16)
            if d:
                mine[p, j] = out
                piece_copy(p, d, mine, theirs, send, recv).start()
            else:
                theirs[p, x] = out
            acc[j] += dot(terms[j, :, at], state, NT)

    def share_out(acc, first_lane, mine, theirs, k):
        acc[x] += gbl[:, first_lane : first_lane + N]
        for j in range(NX):
            mine[:, j, :, :] = acc[j].astype(BF16).reshape(HEADS, T // HEADS, N)

        def send(d, carry):
            shared_copy(d, mine, theirs, k).start()
            return carry

        lax.fori_loop(1, HEADS, send, 0)
        theirs[h] = mine[h]

    def kv_wait(o, carry):
        @pl.when(c >= o)
        def _():
            for copy in kv_copies(o):
                copy.wait_recv()

        return carry

    def turned_block(o, carry):
        rows = pl.ds(pl.multiple_of(o * T, T), T)
        kt[:, rows] = kwin[rows, :].T
        vt[:, rows] = vwin[rows, :].T
        return carry

    def head_pair(i):
        two = 2 * T
        at = lanes(i, two)
        rows = pl.ds(pl.multiple_of(i * two, two), two)
        first = lanes(2 * i, T)
        second = lanes(2 * i + 1, T)
        q2 = qs[rows, :]
        do2 = dos[rows, :]
        scores = dot(kwin[...], q2, NT) * SCALE + bias[...]
        top = jnp.max(scores, axis=0, keepdims=True)
        weights = jnp.exp(scores - top)
        total = jnp.sum(weights, axis=0, keepdims=True)
        out_t = dot(vt[...], weights.astype(BF16)) / total
        out = out_t.T.astype(BF16)
        ao_ref[:, first] = out[:T]
        ao_ref[:, second] = out[T:]
        low = out_t.astype(BF16).astype(F32)
        inner = jnp.sum(low * do2.astype(F32).T, axis=0, keepdims=True)
        prob = weights * (1.0 / total)
        dscore = (prob * (dot(vwin[...], do2, NT) - inner)).astype(BF16)
        pall[:, at] = prob.astype(BF16)
        dsall[:, at] = dscore
        gq = (dot(kt[...], dscore) * SCALE).T.astype(BF16)
        gq_ref[:, first] = gq[:T]
        gq_ref[:, second] = gq[T:]

    def grads_copy(o):
        return remote(dkv_s.at[o], dkv_r.at[o], dkv_ss.at[o], dkv_rs.at[o], ctx_at(-o))

    def grads_block(o, carry):
        rows = pl.ds(pl.multiple_of(o * T, T), T)
        dkv_s[o, :, 0:T] = (dot(dsall[rows, :], qs[...]) * SCALE).astype(BF16)
        dkv_s[o, :, T : 2 * T] = dot(pall[rows, :], dos[...]).astype(BF16)

        @pl.when(c >= o)
        def _():
            grads_copy(o).start()

        return carry

    def mixed(step, carry):
        pf = step - 2 * y
        pb = step - 2 * (NX - 1 - y)
        has_f = (pf >= 0) & (pf < 4)
        has_b = (pb >= 0) & (pb < 4)

        @pl.when(has_f & (y > 0))
        def _():
            forward_copy(pf).wait_recv()

        @pl.when(has_f & (y > 0) & (y < NX - 1))
        def _():
            forward_send(pf)

        @pl.when(has_b & (y < NX - 1))
        def _():
            backward_copy(pb).wait_recv()

        @pl.when(has_b & (y < NX - 1) & (y > 0))
        def _():
            backward_send(pb)

        @pl.when(has_f)
        def _():
            piece(pf, lst, drow, cin, rg, wst, cs, gc_acc, so_s, so_r, of_ss, of_rs)

        @pl.when(has_b)
        def _():
            piece(pb, rst, erow, bin_, bg, wen, xe, gb_acc, gx_s, gx_r, ob_ss, ob_rs)

        @pl.when(pf == 3)
        def _():
            share_out(gc_acc, N, gc_s, gc_r, 1)

        @pl.when(pb == 3)
        def _():
            share_out(gb_acc, 0, gb_s, gb_r, 0)

        @pl.when(step == 1)
        def _():
            lax.fori_loop(1, WIN, kv_wait, 0)
            lax.fori_loop(0, WIN, turned_block, 0)

        @pl.when((step >= 2) & (step < 6))
        def _():
            head_pair(step - 2)

        @pl.when(step == 6)
        def _():
            lax.fori_loop(1, 4, grads_block, 0)

        @pl.when(step == 7)
        def _():
            lax.fori_loop(4, 7, grads_block, 0)

        @pl.when(step == 8)
        def _():
            lax.fori_loop(7, WIN, grads_block, 0)
            own = slice(0, T)
            dkv_own[:, 0:T] = dot(dsall[own, :], qs[...]) * SCALE
            dkv_own[:, T : 2 * T] = dot(pall[own, :], dos[...])

        return carry

    def first_forward(p, carry):
        forward_send(p)
        return carry

    def first_backward(p, carry):
        backward_send(p)
        return carry

    @pl.when(y == 0)
    def _():
        lax.fori_loop(0, 4, first_forward, 0)

    @pl.when(y == NX - 1)
    def _():
        lax.fori_loop(0, 4, first_backward, 0)

    lax.fori_loop(0, 2 * (NX - 1) + 4, mixed, 0)

    def shared_wait(d, carry):
        shared_copy(d, gb_s, gb_r, 0).wait_recv()
        shared_copy(d, gc_s, gc_r, 1).wait_recv()
        return carry

    lax.fori_loop(1, HEADS, shared_wait, 0)
    for k, ref in enumerate((gb_r, gc_r)):
        merged = ref[0].astype(F32)
        for e in range(1, HEADS):
            merged = merged + ref[e].astype(F32)
        gsum[:, k] = merged.astype(BF16)

    def owner_copy(d):
        j = lax.rem(x + d, NX)
        return remote(gsum.at[j], gr.at[x], gg_ss.at[d], gg_rs.at[d], (y * NX + j, h))

    for d in (1, 3, 2):
        owner_copy(d).start()
    gr[x] = gsum[x]

    def pieces_wait(p, carry):
        for d in (1, 3, 2):
            piece_copy(p, d, so_s, so_r, of_ss, of_rs).wait_recv()
            piece_copy(p, d, gx_s, gx_r, ob_ss, ob_rs).wait_recv()
        for s in range(NX):
            at = lanes(s * 4 + p, T)
            so_ref[:, at] = (lo[:, at] + so_r[p, s].astype(F32)).astype(BF16)
            gx_ref[:, at] = (lgx[:, at] + gx_r[p, s].astype(F32)).astype(BF16)
        return carry

    lax.fori_loop(0, 4, pieces_wait, 0)

    def grads_wait(o, carry):
        @pl.when(c + o < CTX)
        def _():
            grads_copy(o).wait_recv()
            dkv_own[...] += dkv_r[o].astype(F32)

        return carry

    lax.fori_loop(1, WIN, grads_wait, 0)
    gk_ref[...] = dkv_own[:, 0:T].astype(BF16)
    gv_ref[...] = dkv_own[:, T : 2 * T].astype(BF16)

    for d in (1, 3, 2):
        owner_copy(d).wait_recv()
    owned = gr[0].astype(F32)
    for e in range(1, NX):
        owned = owned + gr[e].astype(F32)
    gb_ref[...] = owned[0].astype(BF16)
    gc_ref[...] = owned[1].astype(BF16)

    def doc_done(d, carry):
        doc_copy(d).wait_send()
        return carry

    def kv_done(o, carry):
        @pl.when(c + o < CTX)
        def _():
            for copy in kv_copies(o):
                copy.wait_send()

        @pl.when(c >= o)
        def _():
            grads_copy(o).wait_send()

        return carry

    def pieces_done(p, carry):
        for d in (1, 3, 2):
            piece_copy(p, d, so_s, so_r, of_ss, of_rs).wait_send()
            piece_copy(p, d, gx_s, gx_r, ob_ss, ob_rs).wait_send()
        return carry

    def share_done(d, carry):
        for copy in share_copies(d):
            copy.wait_send()
        return carry

    def shared_done(d, carry):
        shared_copy(d, gb_s, gb_r, 0).wait_send()
        shared_copy(d, gc_s, gc_r, 1).wait_send()
        return carry

    def chain_done(p, carry):
        @pl.when(y < NX - 1)
        def _():
            forward_copy(p).wait_send()

        @pl.when(y > 0)
        def _():
            backward_copy(p).wait_send()

        return carry

    lax.fori_loop(1, CTX, doc_done, 0)
    lax.fori_loop(1, WIN, kv_done, 0)
    lax.fori_loop(0, 4, chain_done, 0)
    lax.fori_loop(0, 4, pieces_done, 0)
    lax.fori_loop(1, HEADS, share_done, 0)
    for d in (1, 3, 2):
        owner_copy(d).wait_send()
        for copy in sends[d] + slabs[d]:
            copy.wait_send()
    lax.fori_loop(1, HEADS, shared_done, 0)


def body(q, k, v, do, doc, xs, b, cr, ld, ct):
    vm = pltpu.VMEM
    dma = pltpu.SemaphoreType.DMA
    scratch = [
        vm((T, QL * T), BF16),
        vm((T, QL * T), BF16),
        vm((T, NG * GL), BF16),
        vm((T, N), BF16),
        vm((T, N), BF16),
        vm((T, NG * GL), BF16),
        vm((KEYS, T), BF16),
        vm((KEYS, T), BF16),
        vm((T, KEYS), BF16),
        vm((T, KEYS), BF16),
        vm((CTX, 1, T), jnp.int32),
        vm((KEYS, 2 * T), F32),
        vm((QL * T, T), BF16),
        vm((QL * T, T), BF16),
        vm((KEYS, QL * T), BF16),
        vm((KEYS, QL * T), BF16),
        vm((T, 2 * T), F32),
        vm((WIN, T, 2 * T), BF16),
        vm((WIN, T, 2 * T), BF16),
        vm((NX, T, GL), BF16),
        vm((NX, T, GL), BF16),
        vm((NX, T, N), BF16),
        vm((NX, T, N), BF16),
        vm((32, T), F32),
        vm((NX, 8, T), F32),
        vm((NG, T, T), F32),
        vm((T, NG * GL), F32),
        vm((T, NG * GL), F32),
        vm((T, T), F32),
        vm((T, 2 * N), F32),
        vm((NX, T, GL), F32),
        vm((NX, T, GL), F32),
        vm((NX, T, GL), BF16),
        vm((NX, T, GL), BF16),
        vm((NX, N, GL), F32),
        vm((NX, N, GL), F32),
        vm((NX, N, GL), F32),
        vm((NX, N, GL), F32),
        vm((N, GL), F32),
        vm((N, GL), F32),
        vm((NX, 1, GL), F32),
        vm((NX + 1, 1, GL), F32),
        vm((NX + 1, 1, GL), F32),
        vm((N, GL), BF16),
        vm((4, N, T), BF16),
        vm((N, GL), BF16),
        vm((4, N, T), BF16),
        vm((4, NX, T, T), BF16),
        vm((4, NX, T, T), BF16),
        vm((4, NX, T, T), BF16),
        vm((4, NX, T, T), BF16),
        vm((NX, T, N), F32),
        vm((NX, T, N), F32),
        vm((HEADS, NX, T // HEADS, N), BF16),
        vm((HEADS, NX, T // HEADS, N), BF16),
        vm((HEADS, NX, T // HEADS, N), BF16),
        vm((HEADS, NX, T // HEADS, N), BF16),
        vm((NX, 2, T // HEADS, N), BF16),
        vm((NX, 2, T // HEADS, N), BF16),
        dma((8,)),
        dma((CTX,)),
        dma((CTX,)),
        dma((12,)),
        dma((12,)),
        dma((2 * WIN,)),
        dma((2 * WIN,)),
        dma((4,)),
        dma((4,)),
        dma((4,)),
        dma((4,)),
        dma((8,)),
        dma((8,)),
        dma((16,)),
        dma((16,)),
        dma((16,)),
        dma((16,)),
        dma((16,)),
        dma((16,)),
        dma((4,)),
        dma((4,)),
        dma((WIN,)),
        dma((WIN,)),
        dma((16,)),
        dma((16,)),
    ]
    shape = jax.ShapeDtypeStruct
    outs = (
        shape((T, QL * T), BF16),
        shape((T, NG * GL), BF16),
        shape((T, QL * T), BF16),
        shape((T, T), BF16),
        shape((T, T), BF16),
        shape((T, NG * GL), BF16),
        shape((T // HEADS, N), BF16),
        shape((T // HEADS, N), BF16),
    )
    here = pl.BlockSpec(memory_space=pltpu.VMEM)
    there = pl.BlockSpec(memory_space=pl.ANY)
    results = pl.pallas_call(
        kernel,
        name="packed_layers",
        out_shape=outs,
        in_specs=[there] * 4 + [here] + [there] * 3 + [here, there],
        out_specs=[here] * 8,
        scratch_shapes=scratch,
        compiler_params=pltpu.CompilerParams(
            collective_id=0, has_side_effects=True, vmem_limit_bytes=63 * 1024 * 1024
        ),
    )(q, k, v, do, doc.reshape(1, T), xs, b, cr, ld.T, ct)
    return pl.pallas_call(
        store,
        name="store_results",
        out_shape=outs,
        in_specs=[here] * 8,
        out_specs=[here] * 8,
        compiler_params=pltpu.CompilerParams(vmem_limit_bytes=63 * 1024 * 1024),
    )(*results)


def store(*refs):
    for src, dst in zip(refs[:8], refs[8:]):
        dst[...] = src[...]


def solution(mesh):
    both = P("ctx", "head")
    tokens = P("ctx", None)
    shared = P(("ctx", "head"), None)
    return jax.shard_map(
        body,
        mesh=mesh,
        in_specs=(both, both, both, both, P("ctx"), both, tokens, tokens, both, both),
        out_specs=(both, both, both, both, both, both, shared, shared),
        check_vma=False,
    )
```

```python
import jax
import jax.numpy as jnp
from jax import lax
from jax.experimental import pallas as pl
from jax.experimental.pallas import tpu as pltpu
from jax.sharding import PartitionSpec as P

MESH = pl.DeviceIdType.MESH
F32 = jnp.float32
BF16 = jnp.bfloat16
NEG = -1.0e30
SCALE = 128.0**-0.5

T = 128
CTX = 16
NX = 4
HEADS = 8
QL = 8
WIN = 9
KEYS = WIN * T
N = 256
GL = 512
NG = 4

NN = (((1,), (0,)), ((), ()))
NT = (((1,), (1,)), ((), ()))
TN = (((0,), (0,)), ((), ()))


def dot(a, b, dims=NN):
    return lax.dot_general(a, b, dims, preferred_element_type=F32)


def remote(src, dst, send, recv, device):
    return pltpu.make_async_remote_copy(
        src_ref=src,
        dst_ref=dst,
        send_sem=send,
        recv_sem=recv,
        device_id=device,
        device_id_type=MESH,
    )


def lanes(i, width):
    return pl.ds(pl.multiple_of(i * width, width), width)


def column_of(row):
    return jnp.broadcast_to(row, (T, T)).T


def kernel(
    q_hbm,
    k_hbm,
    v_hbm,
    do_hbm,
    doc_ref,
    x_hbm,
    b_hbm,
    c_hbm,
    ld_ref,
    ct_hbm,
    ao_hbm,
    so_ref,
    gq_hbm,
    gk_ref,
    gv_ref,
    gx_ref,
    gb_ref,
    gc_ref,
    ao_ref,
    gq_ref,
    q_ref,
    do_ref,
    x_ref,
    b_ref,
    c_ref,
    ct_ref,
    kwin,
    vwin,
    kt,
    vt,
    docs,
    bias,
    qs,
    dos,
    pall,
    dsall,
    dkv_own,
    dkv_s,
    dkv_r,
    xg,
    cg,
    bg,
    rg,
    cumr,
    dg,
    ccol,
    lo,
    lgx,
    wsum,
    gbl,
    wst,
    wen,
    xe,
    cs,
    bt,
    rt,
    lst,
    rst,
    lout,
    bout_l,
    prow,
    drow,
    erow,
    cin,
    cout,
    bin_,
    bout,
    so_s,
    gx_s,
    so_r,
    gx_r,
    gb_acc,
    gc_acc,
    gb_s,
    gc_s,
    gb_r,
    gc_r,
    gsum,
    gr,
    in_sem,
    doc_ss,
    doc_rs,
    dc_ss,
    dc_rs,
    xa_ss,
    xa_rs,
    kv_ss,
    kv_rs,
    cf_ss,
    cf_rs,
    cb_ss,
    cb_rs,
    bc_ss,
    bc_rs,
    hd_ss,
    hd_rs,
    of_ss,
    of_rs,
    ob_ss,
    ob_rs,
    gg_ss,
    gg_rs,
    dkv_ss,
    dkv_rs,
    z_ss,
    z_rs,
):
    c = lax.axis_index("ctx")
    h = lax.axis_index("head")
    y = c // NX
    x = lax.rem(c, NX)

    def ctx_at(d):
        return (lax.rem(c + d + CTX, CTX), h)

    def row_at(d):
        return y * NX + lax.rem(x + d, NX)

    barrier = pltpu.get_barrier_semaphore()

    def greet_ctx(d, carry):
        pl.semaphore_signal(barrier, inc=1, device_id=ctx_at(d), device_id_type=MESH)
        return carry

    def greet_head(d, carry):
        pl.semaphore_signal(
            barrier, inc=1, device_id=(c, lax.rem(h + d, HEADS)), device_id_type=MESH
        )
        return carry

    lax.fori_loop(1, CTX, greet_ctx, 0)
    lax.fori_loop(1, HEADS, greet_head, 0)

    own_rows = pl.ds(0, T)
    loads = [
        pltpu.make_async_copy(src, dst, in_sem.at[i])
        for i, (src, dst) in enumerate(
            (
                (b_hbm, b_ref),
                (c_hbm, c_ref),
                (x_hbm, x_ref),
                (ct_hbm, ct_ref),
                (k_hbm, kwin.at[own_rows]),
                (v_hbm, vwin.at[own_rows]),
                (q_hbm, q_ref),
                (do_hbm, do_ref),
            )
        )
    ]
    for load in loads:
        load.start()

    row_i = lax.broadcasted_iota(jnp.int32, (T, T), 0)
    col_i = lax.broadcasted_iota(jnp.int32, (T, T), 1)
    upto = (row_i <= col_i).astype(F32)
    low_half = col_i < 64

    cumr[...] = lax.dot_general(
        ld_ref[...], upto, NN, precision=lax.Precision.HIGHEST, preferred_element_type=F32
    )
    my_slab = pl.ds(pl.multiple_of(h * 16, 16), 16)

    pl.semaphore_wait(barrier, CTX - 1 + HEADS - 1)

    def doc_copy(d):
        return remote(doc_ref, docs.at[c], doc_ss.at[d], doc_rs.at[d], ctx_at(d))

    def doc_send(d, carry):
        doc_copy(d).start()
        return carry

    def slab_copies(d):
        device = (row_at(d), h)
        pairs = ((b_hbm, bg), (c_hbm, rg))
        return [
            remote(
                src.at[my_slab],
                dst.at[x, my_slab],
                bc_ss.at[d * 2 + i],
                bc_rs.at[d * 2 + i],
                device,
            )
            for i, (src, dst) in enumerate(pairs)
        ]

    def share_copies(d):
        device = (c, lax.rem(h + d, HEADS))
        return [
            remote(
                ref.at[:, my_slab, :],
                ref.at[:, my_slab, :],
                hd_ss.at[d * 2 + i],
                hd_rs.at[d * 2 + i],
                device,
            )
            for i, ref in enumerate((bg, rg))
        ]

    def decay_copy(d):
        t = lax.rem(x + d, NX)
        rows = cumr.at[pl.ds(pl.multiple_of(t * 8, 8), 8)]
        return remote(rows, dg.at[x], dc_ss.at[d], dc_rs.at[d], (y * NX + t, h))

    def token_copies(p, d):
        t = lax.rem(x + d, NX)
        src = lanes(t * 4 + p, T)
        dst = lanes(p, T)
        k = (p * NX + d) * 2
        return [
            remote(
                ref.at[:, src],
                out.at[x, :, dst],
                xa_ss.at[k + i],
                xa_rs.at[k + i],
                (y * NX + t, h),
            )
            for i, (ref, out) in enumerate(((x_hbm, xg), (ct_hbm, cg)))
        ]

    slabs = {d: slab_copies(d) for d in (1, 3, 2)}
    decays = {d: decay_copy(d) for d in (1, 3, 2)}
    for d in (1, 3, 2):
        for copy in slabs[d]:
            copy.start()
        decays[d].start()
    lax.fori_loop(1, CTX, doc_send, 0)

    def kv_copies(o):
        rows = pl.ds(pl.multiple_of(o * T, T), T)
        return (
            remote(k_hbm, kwin.at[rows], kv_ss.at[2 * o], kv_rs.at[2 * o], ctx_at(o)),
            remote(v_hbm, vwin.at[rows], kv_ss.at[2 * o + 1], kv_rs.at[2 * o + 1], ctx_at(o)),
        )

    def kv_send(o, carry):
        @pl.when(c + o < CTX)
        def _():
            for copy in kv_copies(o):
                copy.start()

        @pl.when(c < o)
        def _():
            rows = pl.ds(pl.multiple_of(o * T, T), T)
            kwin[rows, :] = jnp.zeros((T, T), BF16)
            vwin[rows, :] = jnp.zeros((T, T), BF16)

        return carry

    lax.fori_loop(1, WIN, kv_send, 0)

    def token_send(p, carry):
        for d in (1, 3, 2):
            for copy in token_copies(p, d):
                copy.start()
        return carry

    lax.fori_loop(0, 4, token_send, 0)

    for load in loads:
        load.wait()
    docs[c] = doc_ref[...]
    xg[x] = x_ref[:, lanes(x, GL)]
    cg[x] = ct_ref[:, lanes(x, GL)]
    bg[x, my_slab, :] = b_ref[my_slab, :]
    rg[x, my_slab, :] = c_ref[my_slab, :]
    dg[x] = cumr[pl.ds(pl.multiple_of(x * 8, 8), 8), :]

    doc_row = doc_ref[...].astype(F32)
    doc_col = column_of(doc_row)
    local_bias = jnp.where((doc_row == doc_col) & (col_i <= row_i), 0.0, NEG)
    gram = dot(c_ref[...], b_ref[...], NT)
    wsum[...] = jnp.zeros((T, T), F32)

    def columns(g, carry):
        rows = cumr[pl.ds(pl.multiple_of(g * 8, 8), 8), :]
        ccol[g] = jnp.concatenate([rows, jnp.zeros((T - 8, T), F32)], axis=0).T
        return carry

    lax.fori_loop(0, NG, columns, 0)
    half_mask = low_half.astype(BF16)
    other_mask = (~low_half).astype(BF16)

    def local_group(g, carry):
        rows = cumr[pl.ds(pl.multiple_of(g * 8, 8), 8), :]
        cols = ccol[g]
        total = wsum[...]
        for p in range(4):
            at = lanes(g * 4 + p, T)
            xp = x_ref[:, at]
            cp = ct_ref[:, at]
            x2 = jnp.concatenate([xp * half_mask, xp * other_mask], axis=0)
            c2 = jnp.concatenate([cp * half_mask, cp * other_mask], axis=0)
            inner = dot(c2, xp, NT)
            mix = []
            for i in range(2):
                j = 2 * p + i
                decay = jnp.exp(cols[:, j : j + 1] - rows[j : j + 1, :] + local_bias)
                mix.append((decay * gram).astype(BF16))
                total = total + decay * inner[i * T : (i + 1) * T]
            lo[:, at] = dot(jnp.concatenate(mix, axis=1), x2)
            lgx[:, at] = dot(jnp.concatenate(mix, axis=0), c2, TN)
        wsum[...] = total
        return carry

    lax.fori_loop(0, NG, local_group, 0)
    weighted = wsum[...].astype(BF16)
    gbl[:, 0:N] = dot(weighted, c_ref[...], TN)
    gbl[:, N : 2 * N] = dot(weighted, b_ref[...])

    for d in (1, 3, 2):
        for copy in slabs[d]:
            copy.wait_recv()

    def share(d, carry):
        for copy in share_copies(d):
            copy.start()
        return carry

    lax.fori_loop(1, HEADS, share, 0)

    def doc_wait(d, carry):
        doc_copy(d).wait_recv()
        return carry

    lax.fori_loop(1, CTX, doc_wait, 0)
    for d in (1, 3, 2):
        decays[d].wait_recv()

    def bias_block(o, carry):
        rows = pl.ds(pl.multiple_of(o * T, T), T)
        kb = lax.rem(c - o + CTX, CTX)
        key_doc = column_of(docs[kb].astype(F32))
        allowed = (key_doc == doc_row) & (kb * T + row_i <= c * T + col_i)
        block = jnp.where(allowed, 0.0, NEG)
        bias[rows, 0:T] = block
        bias[rows, T : 2 * T] = block
        return carry

    def stack_head(i, carry):
        rows = pl.ds(pl.multiple_of(i * T, T), T)
        qs[rows, :] = q_ref[:, lanes(i, T)]
        dos[rows, :] = do_ref[:, lanes(i, T)]
        return carry

    lax.fori_loop(0, WIN, bias_block, 0)
    lax.fori_loop(0, QL, stack_head, 0)

    def weights_of(j, carry):
        cum = dg[j]
        docj = docs[y * NX + j].astype(F32)
        start = jnp.where(docj == docj[:, 0:1], 1.0, 0.0)
        end = jnp.where(docj == docj[:, T - 1 : T], 1.0, 0.0)
        w_start = jnp.exp(cum) * start
        w_end = jnp.exp(cum[:, T - 1 : T] - cum) * end
        table = jnp.concatenate([w_start, w_end, jnp.zeros((T - 16, T), F32)], axis=0).T
        for p in range(4):
            at = slice(p * T, (p + 1) * T)
            ws = jnp.where(low_half, table[:, 2 * p : 2 * p + 1], table[:, 2 * p + 1 : 2 * p + 2])
            we = jnp.where(
                low_half, table[:, 8 + 2 * p : 9 + 2 * p], table[:, 9 + 2 * p : 10 + 2 * p]
            )
            wst[j, :, at] = ws
            wen[j, :, at] = we
            prow[j, :, at] = ws[T - 1 : T, :]
        return carry

    lax.fori_loop(0, NX, weights_of, 0)

    def edge(j, side):
        at = 0 if side == 0 else T - 1
        return docs[j].astype(F32)[:, at : at + 1]

    def linked(first, last, inside):
        same = edge(first, 0) == edge(last, 1)
        return jnp.where(same & inside, 1.0, 0.0)

    base = y * NX
    link = [linked(base, jnp.maximum(base - 1, 0), y > 0)]
    link += [linked(base + j, base + j - 1, y >= 0) for j in range(1, NX)]
    link += [linked(jnp.minimum(base + NX, CTX - 1), base + NX - 1, y < NX - 1)]
    wide = [jnp.broadcast_to(value, (1, GL)) for value in link]

    drow[0] = wide[0]
    for j in range(NX - 1):
        drow[j + 1] = wide[j + 1] * prow[j] * drow[j]
    drow[NX] = prow[NX - 1] * drow[NX - 1]
    erow[NX - 1] = wide[NX]
    for j in range(NX - 1, 0, -1):
        erow[j - 1] = wide[j] * prow[j] * erow[j]
    erow[NX] = prow[0] * erow[0]

    @pl.when(y == 0)
    def _():
        cin[...] = jnp.zeros((N, GL), BF16)

    @pl.when(y == NX - 1)
    def _():
        bin_[...] = jnp.zeros((N, GL), BF16)

    def kv_wait(o, carry):
        @pl.when(c >= o)
        def _():
            for copy in kv_copies(o):
                copy.wait_recv()

        return carry

    def turned_block(o, carry):
        rows = pl.ds(pl.multiple_of(o * T, T), T)
        kt[:, rows] = kwin[rows, :].T
        vt[:, rows] = vwin[rows, :].T
        return carry

    def head_pair(i, carry):
        two = 2 * T
        at = lanes(i, two)
        rows = pl.ds(pl.multiple_of(i * two, two), two)
        first = lanes(2 * i, T)
        second = lanes(2 * i + 1, T)
        q2 = qs[rows, :]
        do2 = dos[rows, :]
        scores = dot(kwin[...], q2, NT) * SCALE + bias[...]
        top = jnp.max(scores, axis=0, keepdims=True)
        weights = jnp.exp(scores - top)
        total = jnp.sum(weights, axis=0, keepdims=True)
        out_t = dot(vt[...], weights.astype(BF16)) / total
        out = out_t.T.astype(BF16)
        ao_ref[:, first] = out[:T]
        ao_ref[:, second] = out[T:]
        low = out_t.astype(BF16).astype(F32)
        inner = jnp.sum(low * do2.astype(F32).T, axis=0, keepdims=True)
        prob = weights * (1.0 / total)
        dscore = (prob * (dot(vwin[...], do2, NT) - inner)).astype(BF16)
        pall[:, at] = prob.astype(BF16)
        dsall[:, at] = dscore
        gq = (dot(kt[...], dscore) * SCALE).T.astype(BF16)
        gq_ref[:, first] = gq[:T]
        gq_ref[:, second] = gq[T:]
        return carry

    def grads_copy(o):
        return remote(dkv_s.at[o], dkv_r.at[o], dkv_ss.at[o], dkv_rs.at[o], ctx_at(-o))

    def grads_block(o, carry):
        rows = pl.ds(pl.multiple_of(o * T, T), T)
        dkv_s[o, :, 0:T] = (dot(dsall[rows, :], qs[...]) * SCALE).astype(BF16)
        dkv_s[o, :, T : 2 * T] = dot(pall[rows, :], dos[...]).astype(BF16)
        return carry

    def grads_send(o, carry):
        @pl.when(c >= o)
        def _():
            grads_copy(o).start()

        return carry

    lax.fori_loop(1, WIN, kv_wait, 0)
    lax.fori_loop(0, WIN, turned_block, 0)
    def share_wait(d, carry):
        for copy in share_copies(d):
            copy.wait_recv()
        return carry

    lax.fori_loop(1, HEADS, share_wait, 0)
    for j in range(NX):
        bt[j] = bg[j].T
        rt[j] = rg[j].T
        gc_acc[j] = jnp.zeros((T, N), F32)
        gb_acc[j] = jnp.zeros((T, N), F32)

    def block_sums(p):
        at = lanes(p, T)
        for d in (1, 3, 2):
            for copy in token_copies(p, d):
                copy.wait_recv()
        value = jnp.zeros((N, T), F32)
        for j in range(NX):
            term = (xg[j, :, at].astype(F32) * wen[j, :, at]).astype(BF16)
            xe[j, :, at] = term
            lst[j, :, at] = value
            value = prow[j, :, at] * value + dot(bt[j], term)
            if j < NX - 1:
                value = link[j + 1] * value
        lout[:, at] = value
        value = jnp.zeros((N, T), F32)
        for j in range(NX - 1, -1, -1):
            term = (cg[j, :, at].astype(F32) * wst[j, :, at]).astype(BF16)
            cs[j, :, at] = term
            rst[j, :, at] = value
            value = prow[j, :, at] * value + dot(rt[j], term)
            if j > 0:
                value = link[j] * value
        bout_l[:, at] = value

    def forward_copy(p):
        device = (lax.rem(c + NX, CTX), h)
        return remote(cout.at[p], cin.at[:, lanes(p, T)], cf_ss.at[p], cf_rs.at[p], device)

    def backward_copy(p):
        device = (lax.rem(c + CTX - NX, CTX), h)
        return remote(bout.at[p], bin_.at[:, lanes(p, T)], cb_ss.at[p], cb_rs.at[p], device)

    def forward_send(p):
        at = lanes(p, T)
        value = lout[:, at] + drow[NX, :, at] * cin[:, at].astype(F32)
        cout[p] = value.astype(BF16)
        forward_copy(p).start()

    def backward_send(p):
        at = lanes(p, T)
        value = bout_l[:, at] + erow[NX, :, at] * bin_[:, at].astype(F32)
        bout[p] = value.astype(BF16)
        backward_copy(p).start()

    def piece_copy(p, d, mine, theirs, send, recv):
        j = lax.rem(x + d, NX)
        k = p * NX + d
        return remote(mine.at[p, j], theirs.at[p, x], send.at[k], recv.at[k], (y * NX + j, h))

    def shared_copy(d, mine, theirs, k):
        e = lax.rem(h + d, HEADS)
        k = 2 * d + k
        return remote(mine.at[e], theirs.at[h], z_ss.at[k], z_rs.at[k], (c, e))

    def piece(p, local, scale, carried, proj, weight, terms, acc, mine, theirs, send, recv):
        at = lanes(p, T)
        value = carried[:, at].astype(F32)
        for d in (1, 3, 2, 0):
            j = lax.rem(x + d, NX)
            state = (local[j, :, at] + scale[j, :, at] * value).astype(BF16)
            out = (dot(proj[j], state) * weight[j, :, at]).astype(BF16)
            if d:
                mine[p, j] = out
                piece_copy(p, d, mine, theirs, send, recv).start()
            else:
                theirs[p, x] = out
            acc[j] += dot(terms[j, :, at], state, NT)

    def share_out(acc, first_lane, mine, theirs, k):
        acc[x] += gbl[:, first_lane : first_lane + N]
        for j in range(NX):
            mine[:, j, :, :] = acc[j].astype(BF16).reshape(HEADS, T // HEADS, N)

        def send(d, carry):
            shared_copy(d, mine, theirs, k).start()
            return carry

        lax.fori_loop(1, HEADS, send, 0)
        theirs[h] = mine[h]

    early = [
        pltpu.make_async_copy(ao_ref, ao_hbm, in_sem.at[0]),
        pltpu.make_async_copy(gq_ref, gq_hbm, in_sem.at[1]),
    ]

    def mixed(step, carry):
        pf = step - y
        pb = step - (NX - 1 - y)
        has_f = (pf >= 0) & (pf < 4)
        has_b = (pb >= 0) & (pb < 4)

        @pl.when(step < 4)
        def _():
            block_sums(step)

        @pl.when(has_f & (y > 0))
        def _():
            forward_copy(pf).wait_recv()

        @pl.when(has_f & (y < NX - 1))
        def _():
            forward_send(pf)

        @pl.when(has_b & (y < NX - 1))
        def _():
            backward_copy(pb).wait_recv()

        @pl.when(has_b & (y > 0))
        def _():
            backward_send(pb)

        @pl.when(has_f)
        def _():
            piece(pf, lst, drow, cin, rg, wst, cs, gc_acc, so_s, so_r, of_ss, of_rs)

        @pl.when(has_b)
        def _():
            piece(pb, rst, erow, bin_, bg, wen, xe, gb_acc, gx_s, gx_r, ob_ss, ob_rs)

        @pl.when(pf == 3)
        def _():
            share_out(gc_acc, N, gc_s, gc_r, 1)

        @pl.when(pb == 3)
        def _():
            share_out(gb_acc, 0, gb_s, gb_r, 0)

        @pl.when(step < QL // 2)
        def _():
            head_pair(step, 0)

        @pl.when(step == 4)
        def _():
            for copy in early:
                copy.start()
            lax.fori_loop(1, 5, grads_block, 0)

        @pl.when(step == 5)
        def _():
            lax.fori_loop(5, WIN, grads_block, 0)
            own = slice(0, T)
            dkv_own[:, 0:T] = dot(dsall[own, :], qs[...]) * SCALE
            dkv_own[:, T : 2 * T] = dot(pall[own, :], dos[...])

        return carry

    lax.fori_loop(0, NX - 1 + 4, mixed, 0)

    lax.fori_loop(1, WIN, grads_send, 0)

    def shared_wait(d, carry):
        shared_copy(d, gb_s, gb_r, 0).wait_recv()
        shared_copy(d, gc_s, gc_r, 1).wait_recv()
        return carry

    lax.fori_loop(1, HEADS, shared_wait, 0)
    for k, ref in enumerate((gb_r, gc_r)):
        merged = ref[0].astype(F32)
        for e in range(1, HEADS):
            merged = merged + ref[e].astype(F32)
        gsum[:, k] = merged.astype(BF16)

    def owner_copy(d):
        j = lax.rem(x + d, NX)
        return remote(gsum.at[j], gr.at[x], gg_ss.at[d], gg_rs.at[d], (y * NX + j, h))

    for d in (1, 3, 2):
        owner_copy(d).start()
    gr[x] = gsum[x]

    def pieces_wait(p, carry):
        for d in (1, 3, 2):
            piece_copy(p, d, so_s, so_r, of_ss, of_rs).wait_recv()
            piece_copy(p, d, gx_s, gx_r, ob_ss, ob_rs).wait_recv()
        for s in range(NX):
            at = lanes(s * 4 + p, T)
            so_ref[:, at] = (lo[:, at] + so_r[p, s].astype(F32)).astype(BF16)
            gx_ref[:, at] = (lgx[:, at] + gx_r[p, s].astype(F32)).astype(BF16)
        return carry

    lax.fori_loop(0, 4, pieces_wait, 0)

    def grads_wait(o, carry):
        @pl.when(c + o < CTX)
        def _():
            grads_copy(o).wait_recv()
            dkv_own[...] += dkv_r[o].astype(F32)

        return carry

    lax.fori_loop(1, WIN, grads_wait, 0)
    gk_ref[...] = dkv_own[:, 0:T].astype(BF16)
    gv_ref[...] = dkv_own[:, T : 2 * T].astype(BF16)

    for d in (1, 3, 2):
        owner_copy(d).wait_recv()
    owned = gr[0].astype(F32)
    for e in range(1, NX):
        owned = owned + gr[e].astype(F32)
    gb_ref[...] = owned[0].astype(BF16)
    gc_ref[...] = owned[1].astype(BF16)

    for copy in early:
        copy.wait()

    def doc_done(d, carry):
        doc_copy(d).wait_send()
        return carry

    def kv_done(o, carry):
        @pl.when(c + o < CTX)
        def _():
            for copy in kv_copies(o):
                copy.wait_send()

        @pl.when(c >= o)
        def _():
            grads_copy(o).wait_send()

        return carry

    def pieces_done(p, carry):
        for d in (1, 3, 2):
            for copy in token_copies(p, d):
                copy.wait_send()
            piece_copy(p, d, so_s, so_r, of_ss, of_rs).wait_send()
            piece_copy(p, d, gx_s, gx_r, ob_ss, ob_rs).wait_send()
        return carry

    def share_done(d, carry):
        for copy in share_copies(d):
            copy.wait_send()
        return carry

    def shared_done(d, carry):
        shared_copy(d, gb_s, gb_r, 0).wait_send()
        shared_copy(d, gc_s, gc_r, 1).wait_send()
        return carry

    def chain_done(p, carry):
        @pl.when(y < NX - 1)
        def _():
            forward_copy(p).wait_send()

        @pl.when(y > 0)
        def _():
            backward_copy(p).wait_send()

        return carry

    lax.fori_loop(1, CTX, doc_done, 0)
    lax.fori_loop(1, WIN, kv_done, 0)
    lax.fori_loop(0, 4, chain_done, 0)
    lax.fori_loop(0, 4, pieces_done, 0)
    lax.fori_loop(1, HEADS, share_done, 0)
    for d in (1, 3, 2):
        owner_copy(d).wait_send()
        decays[d].wait_send()
        for copy in slabs[d]:
            copy.wait_send()
    lax.fori_loop(1, HEADS, shared_done, 0)


def body(q, k, v, do, doc, xs, b, cr, ld, ct):
    vm = pltpu.VMEM
    dma = pltpu.SemaphoreType.DMA
    scratch = [
        vm((T, QL * T), BF16),
        vm((T, QL * T), BF16),
        vm((T, QL * T), BF16),
        vm((T, QL * T), BF16),
        vm((T, NG * GL), BF16),
        vm((T, N), BF16),
        vm((T, N), BF16),
        vm((T, NG * GL), BF16),
        vm((KEYS, T), BF16),
        vm((KEYS, T), BF16),
        vm((T, KEYS), BF16),
        vm((T, KEYS), BF16),
        vm((CTX, 1, T), jnp.int32),
        vm((KEYS, 2 * T), F32),
        vm((QL * T, T), BF16),
        vm((QL * T, T), BF16),
        vm((KEYS, QL * T), BF16),
        vm((KEYS, QL * T), BF16),
        vm((T, 2 * T), F32),
        vm((WIN, T, 2 * T), BF16),
        vm((WIN, T, 2 * T), BF16),
        vm((NX, T, GL), BF16),
        vm((NX, T, GL), BF16),
        vm((NX, T, N), BF16),
        vm((NX, T, N), BF16),
        vm((32, T), F32),
        vm((NX, 8, T), F32),
        vm((NG, T, T), F32),
        vm((T, NG * GL), F32),
        vm((T, NG * GL), F32),
        vm((T, T), F32),
        vm((T, 2 * N), F32),
        vm((NX, T, GL), F32),
        vm((NX, T, GL), F32),
        vm((NX, T, GL), BF16),
        vm((NX, T, GL), BF16),
        vm((NX, N, T), BF16),
        vm((NX, N, T), BF16),
        vm((NX, N, GL), F32),
        vm((NX, N, GL), F32),
        vm((N, GL), F32),
        vm((N, GL), F32),
        vm((NX, 1, GL), F32),
        vm((NX + 1, 1, GL), F32),
        vm((NX + 1, 1, GL), F32),
        vm((N, GL), BF16),
        vm((4, N, T), BF16),
        vm((N, GL), BF16),
        vm((4, N, T), BF16),
        vm((4, NX, T, T), BF16),
        vm((4, NX, T, T), BF16),
        vm((4, NX, T, T), BF16),
        vm((4, NX, T, T), BF16),
        vm((NX, T, N), F32),
        vm((NX, T, N), F32),
        vm((HEADS, NX, T // HEADS, N), BF16),
        vm((HEADS, NX, T // HEADS, N), BF16),
        vm((HEADS, NX, T // HEADS, N), BF16),
        vm((HEADS, NX, T // HEADS, N), BF16),
        vm((NX, 2, T // HEADS, N), BF16),
        vm((NX, 2, T // HEADS, N), BF16),
        dma((8,)),
        dma((CTX,)),
        dma((CTX,)),
        dma((4,)),
        dma((4,)),
        dma((32,)),
        dma((32,)),
        dma((2 * WIN,)),
        dma((2 * WIN,)),
        dma((4,)),
        dma((4,)),
        dma((4,)),
        dma((4,)),
        dma((8,)),
        dma((8,)),
        dma((16,)),
        dma((16,)),
        dma((16,)),
        dma((16,)),
        dma((16,)),
        dma((16,)),
        dma((4,)),
        dma((4,)),
        dma((WIN,)),
        dma((WIN,)),
        dma((16,)),
        dma((16,)),
    ]
    shape = jax.ShapeDtypeStruct
    outs = (
        shape((T, QL * T), BF16),
        shape((T, NG * GL), BF16),
        shape((T, QL * T), BF16),
        shape((T, T), BF16),
        shape((T, T), BF16),
        shape((T, NG * GL), BF16),
        shape((T // HEADS, N), BF16),
        shape((T // HEADS, N), BF16),
    )
    here = pl.BlockSpec(memory_space=pltpu.VMEM)
    there = pl.BlockSpec(memory_space=pl.ANY)
    results = pl.pallas_call(
        kernel,
        name="packed_layers",
        out_shape=outs,
        in_specs=[there] * 4 + [here] + [there] * 3 + [here, there],
        out_specs=[there, here, there] + [here] * 5,
        scratch_shapes=scratch,
        compiler_params=pltpu.CompilerParams(
            collective_id=0, has_side_effects=True, vmem_limit_bytes=63 * 1024 * 1024
        ),
    )(q, k, v, do, doc.reshape(1, T), xs, b, cr, ld.T, ct)
    return pl.pallas_call(
        store,
        name="store_results",
        out_shape=outs,
        in_specs=[here] * 8,
        out_specs=[here] * 8,
        compiler_params=pltpu.CompilerParams(vmem_limit_bytes=63 * 1024 * 1024),
    )(*results)


def store(*refs):
    for src, dst in zip(refs[:8], refs[8:]):
        dst[...] = src[...]


def solution(mesh):
    both = P("ctx", "head")
    tokens = P("ctx", None)
    shared = P(("ctx", "head"), None)
    return jax.shard_map(
        body,
        mesh=mesh,
        in_specs=(both, both, both, both, P("ctx"), both, tokens, tokens, both, both),
        out_specs=(both, both, both, both, both, both, shared, shared),
        check_vma=False,
    )
```

```python
import jax
import jax.numpy as jnp
from jax import lax
from jax.experimental import pallas as pl
from jax.experimental.pallas import tpu as pltpu
from jax.sharding import PartitionSpec as P

MESH = pl.DeviceIdType.MESH
F32 = jnp.float32
BF16 = jnp.bfloat16
NEG = -1.0e30
SCALE = 128.0**-0.5

T = 128
CTX = 16
NX = 4
HEADS = 8
QL = 8
WIN = 9
KEYS = WIN * T
N = 256
GL = 512
NG = 4

NN = (((1,), (0,)), ((), ()))
NT = (((1,), (1,)), ((), ()))
TN = (((0,), (0,)), ((), ()))


def dot(a, b, dims=NN):
    return lax.dot_general(a, b, dims, preferred_element_type=F32)


def remote(src, dst, send, recv, device):
    return pltpu.make_async_remote_copy(
        src_ref=src,
        dst_ref=dst,
        send_sem=send,
        recv_sem=recv,
        device_id=device,
        device_id_type=MESH,
    )


def lanes(i, width):
    return pl.ds(pl.multiple_of(i * width, width), width)


def column_of(row):
    return jnp.broadcast_to(row, (T, T)).T


def kernel(
    q_hbm,
    k_hbm,
    v_hbm,
    do_hbm,
    doc_ref,
    x_hbm,
    b_hbm,
    c_hbm,
    ld_ref,
    ct_hbm,
    ao_hbm,
    so_ref,
    gq_hbm,
    gk_ref,
    gv_ref,
    gx_ref,
    gb_ref,
    gc_ref,
    ao_ref,
    gq_ref,
    q_ref,
    do_ref,
    x_ref,
    b_ref,
    c_ref,
    ct_ref,
    kwin,
    vwin,
    kt,
    vt,
    docs,
    bias,
    qs,
    dos,
    pall,
    dsall,
    dkv_own,
    dkv_s,
    dkv_r,
    up_sum,
    up_s,
    up_r,
    xg,
    cg,
    bg,
    rg,
    cumr,
    dg,
    ccol,
    lo,
    lgx,
    wsum,
    gbl,
    wst,
    wen,
    xe,
    cs,
    bt,
    rt,
    lst,
    rst,
    lout,
    bout_l,
    prow,
    drow,
    erow,
    cin,
    cout,
    bin_,
    bout,
    so_s,
    gx_s,
    so_r,
    gx_r,
    gb_acc,
    gc_acc,
    gb_s,
    gc_s,
    gb_r,
    gc_r,
    gsum,
    gr,
    in_sem,
    doc_ss,
    doc_rs,
    dc_ss,
    dc_rs,
    xa_ss,
    xa_rs,
    kv_ss,
    kv_rs,
    cf_ss,
    cf_rs,
    cb_ss,
    cb_rs,
    bc_ss,
    bc_rs,
    hd_ss,
    hd_rs,
    of_ss,
    of_rs,
    ob_ss,
    ob_rs,
    gg_ss,
    gg_rs,
    dkv_ss,
    dkv_rs,
    up_ss,
    up_rs,
    z_ss,
    z_rs,
):
    c = lax.axis_index("ctx")
    h = lax.axis_index("head")
    y = c // NX
    x = lax.rem(c, NX)

    def ctx_at(d):
        return (lax.rem(c + d + CTX, CTX), h)

    def row_at(d):
        return y * NX + lax.rem(x + d, NX)

    barrier = pltpu.get_barrier_semaphore()

    def greet_ctx(d, carry):
        pl.semaphore_signal(barrier, inc=1, device_id=ctx_at(d), device_id_type=MESH)
        return carry

    def greet_head(d, carry):
        pl.semaphore_signal(
            barrier, inc=1, device_id=(c, lax.rem(h + d, HEADS)), device_id_type=MESH
        )
        return carry

    lax.fori_loop(1, CTX, greet_ctx, 0)
    lax.fori_loop(1, HEADS, greet_head, 0)

    own_rows = pl.ds(0, T)
    loads = [
        pltpu.make_async_copy(src, dst, in_sem.at[i])
        for i, (src, dst) in enumerate(
            (
                (b_hbm, b_ref),
                (c_hbm, c_ref),
                (x_hbm, x_ref),
                (ct_hbm, ct_ref),
                (k_hbm, kwin.at[own_rows]),
                (v_hbm, vwin.at[own_rows]),
                (q_hbm, q_ref),
                (do_hbm, do_ref),
            )
        )
    ]
    for load in loads:
        load.start()

    row_i = lax.broadcasted_iota(jnp.int32, (T, T), 0)
    col_i = lax.broadcasted_iota(jnp.int32, (T, T), 1)
    upto = (row_i <= col_i).astype(F32)
    low_half = col_i < 64

    cumr[...] = lax.dot_general(
        ld_ref[...], upto, NN, precision=lax.Precision.HIGHEST, preferred_element_type=F32
    )
    my_slab = pl.ds(pl.multiple_of(h * 16, 16), 16)

    pl.semaphore_wait(barrier, CTX - 1 + HEADS - 1)

    def doc_copy(d):
        return remote(doc_ref, docs.at[c], doc_ss.at[d], doc_rs.at[d], ctx_at(d))

    def doc_send(d, carry):
        doc_copy(d).start()
        return carry

    def slab_copies(d):
        device = (row_at(d), h)
        pairs = ((b_hbm, bg), (c_hbm, rg))
        return [
            remote(
                src.at[my_slab],
                dst.at[x, my_slab],
                bc_ss.at[d * 2 + i],
                bc_rs.at[d * 2 + i],
                device,
            )
            for i, (src, dst) in enumerate(pairs)
        ]

    def share_copies(d):
        device = (c, lax.rem(h + d, HEADS))
        return [
            remote(
                ref.at[:, my_slab, :],
                ref.at[:, my_slab, :],
                hd_ss.at[d * 2 + i],
                hd_rs.at[d * 2 + i],
                device,
            )
            for i, ref in enumerate((bg, rg))
        ]

    def decay_copy(d):
        t = lax.rem(x + d, NX)
        rows = cumr.at[pl.ds(pl.multiple_of(t * 8, 8), 8)]
        return remote(rows, dg.at[x], dc_ss.at[d], dc_rs.at[d], (y * NX + t, h))

    def token_copies(p, d):
        t = lax.rem(x + d, NX)
        src = lanes(t * 4 + p, T)
        dst = lanes(p, T)
        k = (p * NX + d) * 2
        return [
            remote(
                ref.at[:, src],
                out.at[x, :, dst],
                xa_ss.at[k + i],
                xa_rs.at[k + i],
                (y * NX + t, h),
            )
            for i, (ref, out) in enumerate(((x_hbm, xg), (ct_hbm, cg)))
        ]

    slabs = {d: slab_copies(d) for d in (1, 3, 2)}
    decays = {d: decay_copy(d) for d in (1, 3, 2)}
    for d in (1, 3, 2):
        for copy in slabs[d]:
            copy.start()
        decays[d].start()
    lax.fori_loop(1, CTX, doc_send, 0)

    def kv_copies(o):
        rows = pl.ds(pl.multiple_of(o * T, T), T)
        return (
            remote(k_hbm, kwin.at[rows], kv_ss.at[2 * o], kv_rs.at[2 * o], ctx_at(o)),
            remote(v_hbm, vwin.at[rows], kv_ss.at[2 * o + 1], kv_rs.at[2 * o + 1], ctx_at(o)),
        )

    def kv_send(o, carry):
        @pl.when(c + o < CTX)
        def _():
            for copy in kv_copies(o):
                copy.start()

        @pl.when(c < o)
        def _():
            rows = pl.ds(pl.multiple_of(o * T, T), T)
            kwin[rows, :] = jnp.zeros((T, T), BF16)
            vwin[rows, :] = jnp.zeros((T, T), BF16)

        return carry

    lax.fori_loop(1, WIN, kv_send, 0)

    def token_send(p, carry):
        for d in (1, 3, 2):
            for copy in token_copies(p, d):
                copy.start()
        return carry

    lax.fori_loop(0, 4, token_send, 0)

    for load in loads:
        load.wait()
    docs[c] = doc_ref[...]
    xg[x] = x_ref[:, lanes(x, GL)]
    cg[x] = ct_ref[:, lanes(x, GL)]
    bg[x, my_slab, :] = b_ref[my_slab, :]
    rg[x, my_slab, :] = c_ref[my_slab, :]
    dg[x] = cumr[pl.ds(pl.multiple_of(x * 8, 8), 8), :]

    for d in (1, 3, 2):
        for copy in slabs[d]:
            copy.wait_recv()

    def share(d, carry):
        for copy in share_copies(d):
            copy.start()
        return carry

    lax.fori_loop(1, HEADS, share, 0)

    doc_row = doc_ref[...].astype(F32)
    doc_col = column_of(doc_row)
    local_bias = jnp.where((doc_row == doc_col) & (col_i <= row_i), 0.0, NEG)
    gram = dot(c_ref[...], b_ref[...], NT)
    wsum[...] = jnp.zeros((T, T), F32)

    def columns(g, carry):
        rows = cumr[pl.ds(pl.multiple_of(g * 8, 8), 8), :]
        ccol[g] = jnp.concatenate([rows, jnp.zeros((T - 8, T), F32)], axis=0).T
        return carry

    lax.fori_loop(0, NG, columns, 0)
    half_mask = low_half.astype(BF16)
    other_mask = (~low_half).astype(BF16)

    def local_group(g, carry):
        rows = cumr[pl.ds(pl.multiple_of(g * 8, 8), 8), :]
        cols = ccol[g]
        total = wsum[...]
        for p in range(4):
            at = lanes(g * 4 + p, T)
            xp = x_ref[:, at]
            cp = ct_ref[:, at]
            x2 = jnp.concatenate([xp * half_mask, xp * other_mask], axis=0)
            c2 = jnp.concatenate([cp * half_mask, cp * other_mask], axis=0)
            inner = dot(c2, xp, NT)
            mix = []
            for i in range(2):
                j = 2 * p + i
                decay = jnp.exp(cols[:, j : j + 1] - rows[j : j + 1, :] + local_bias)
                mix.append((decay * gram).astype(BF16))
                total = total + decay * inner[i * T : (i + 1) * T]
            lo[:, at] = dot(jnp.concatenate(mix, axis=1), x2)
            lgx[:, at] = dot(jnp.concatenate(mix, axis=0), c2, TN)
        wsum[...] = total
        return carry

    lax.fori_loop(0, NG, local_group, 0)
    weighted = wsum[...].astype(BF16)
    gbl[:, 0:N] = dot(weighted, c_ref[...], TN)
    gbl[:, N : 2 * N] = dot(weighted, b_ref[...])

    def doc_wait(d, carry):
        doc_copy(d).wait_recv()
        return carry

    lax.fori_loop(1, CTX, doc_wait, 0)
    for d in (1, 3, 2):
        decays[d].wait_recv()

    def bias_block(o, carry):
        rows = pl.ds(pl.multiple_of(o * T, T), T)
        kb = lax.rem(c - o + CTX, CTX)
        key_doc = column_of(docs[kb].astype(F32))
        allowed = (key_doc == doc_row) & (kb * T + row_i <= c * T + col_i)
        block = jnp.where(allowed, 0.0, NEG)
        bias[rows, 0:T] = block
        bias[rows, T : 2 * T] = block
        return carry

    def stack_head(i, carry):
        rows = pl.ds(pl.multiple_of(i * T, T), T)
        qs[rows, :] = q_ref[:, lanes(i, T)]
        dos[rows, :] = do_ref[:, lanes(i, T)]
        return carry

    lax.fori_loop(0, WIN, bias_block, 0)
    lax.fori_loop(0, QL, stack_head, 0)

    def weights_of(j, carry):
        cum = dg[j]
        docj = docs[y * NX + j].astype(F32)
        start = jnp.where(docj == docj[:, 0:1], 1.0, 0.0)
        end = jnp.where(docj == docj[:, T - 1 : T], 1.0, 0.0)
        w_start = jnp.exp(cum) * start
        w_end = jnp.exp(cum[:, T - 1 : T] - cum) * end
        table = jnp.concatenate([w_start, w_end, jnp.zeros((T - 16, T), F32)], axis=0).T
        for p in range(4):
            at = slice(p * T, (p + 1) * T)
            ws = jnp.where(low_half, table[:, 2 * p : 2 * p + 1], table[:, 2 * p + 1 : 2 * p + 2])
            we = jnp.where(
                low_half, table[:, 8 + 2 * p : 9 + 2 * p], table[:, 9 + 2 * p : 10 + 2 * p]
            )
            wst[j, :, at] = ws
            wen[j, :, at] = we
            prow[j, :, at] = ws[T - 1 : T, :]
        return carry

    lax.fori_loop(0, NX, weights_of, 0)

    def edge(j, side):
        at = 0 if side == 0 else T - 1
        return docs[j].astype(F32)[:, at : at + 1]

    def linked(first, last, inside):
        same = edge(first, 0) == edge(last, 1)
        return jnp.where(same & inside, 1.0, 0.0)

    base = y * NX
    link = [linked(base, jnp.maximum(base - 1, 0), y > 0)]
    link += [linked(base + j, base + j - 1, y >= 0) for j in range(1, NX)]
    link += [linked(jnp.minimum(base + NX, CTX - 1), base + NX - 1, y < NX - 1)]
    wide = [jnp.broadcast_to(value, (1, GL)) for value in link]

    drow[0] = wide[0]
    for j in range(NX - 1):
        drow[j + 1] = wide[j + 1] * prow[j] * drow[j]
    drow[NX] = prow[NX - 1] * drow[NX - 1]
    erow[NX - 1] = wide[NX]
    for j in range(NX - 1, 0, -1):
        erow[j - 1] = wide[j] * prow[j] * erow[j]
    erow[NX] = prow[0] * erow[0]

    @pl.when(y == 0)
    def _():
        cin[...] = jnp.zeros((N, GL), BF16)

    @pl.when(y == NX - 1)
    def _():
        bin_[...] = jnp.zeros((N, GL), BF16)

    def kv_wait(o, carry):
        @pl.when(c >= o)
        def _():
            for copy in kv_copies(o):
                copy.wait_recv()

        return carry

    def turned_block(o, carry):
        rows = pl.ds(pl.multiple_of(o * T, T), T)
        kt[:, rows] = kwin[rows, :].T
        vt[:, rows] = vwin[rows, :].T
        return carry

    def head_pair(i, carry):
        two = 2 * T
        at = lanes(i, two)
        rows = pl.ds(pl.multiple_of(i * two, two), two)
        first = lanes(2 * i, T)
        second = lanes(2 * i + 1, T)
        q2 = qs[rows, :]
        do2 = dos[rows, :]
        scores = dot(kwin[...], q2, NT) * SCALE + bias[...]
        top = jnp.max(scores, axis=0, keepdims=True)
        weights = jnp.exp(scores - top)
        total = jnp.sum(weights, axis=0, keepdims=True)
        out_t = dot(vt[...], weights.astype(BF16)) / total
        out = out_t.T.astype(BF16)
        ao_ref[:, first] = out[:T]
        ao_ref[:, second] = out[T:]
        low = out_t.astype(BF16).astype(F32)
        inner = jnp.sum(low * do2.astype(F32).T, axis=0, keepdims=True)
        prob = weights * (1.0 / total)
        dscore = (prob * (dot(vwin[...], do2, NT) - inner)).astype(BF16)
        pall[:, at] = prob.astype(BF16)
        dsall[:, at] = dscore
        gq = (dot(kt[...], dscore) * SCALE).T.astype(BF16)
        gq_ref[:, first] = gq[:T]
        gq_ref[:, second] = gq[T:]
        return carry

    def row_grads(d):
        t = lax.rem(x + d, NX)
        device = (y * NX + t, h)
        blocks = (NX + x - t, lax.rem(2 * NX + x - t, 2 * NX))
        return [
            remote(
                dkv_s.at[o],
                dkv_r.at[2 * d + i],
                dkv_ss.at[2 * d + i],
                dkv_rs.at[2 * d + i],
                device,
            )
            for i, o in enumerate(blocks)
        ]

    def column_grads(r):
        device = (lax.rem(c + CTX - r * NX, CTX), h)
        return remote(up_s.at[r], up_r.at[r], up_ss.at[r], up_rs.at[r], device)

    def grads_block(o, carry):
        rows = pl.ds(pl.multiple_of(o * T, T), T)
        dkv_s[o, :, 0:T] = (dot(dsall[rows, :], qs[...]) * SCALE).astype(BF16)
        dkv_s[o, :, T : 2 * T] = dot(pall[rows, :], dos[...]).astype(BF16)
        return carry

    def share_wait(d, carry):
        for copy in share_copies(d):
            copy.wait_recv()
        return carry

    lax.fori_loop(1, HEADS, share_wait, 0)
    for j in range(NX):
        bt[j] = bg[j].T
        rt[j] = rg[j].T
        gc_acc[j] = jnp.zeros((T, N), F32)
        gb_acc[j] = jnp.zeros((T, N), F32)

    def block_sums(p):
        at = lanes(p, T)
        for d in (1, 3, 2):
            for copy in token_copies(p, d):
                copy.wait_recv()
        value = jnp.zeros((N, T), F32)
        for j in range(NX):
            term = (xg[j, :, at].astype(F32) * wen[j, :, at]).astype(BF16)
            xe[j, :, at] = term
            lst[j, :, at] = value
            value = prow[j, :, at] * value + dot(bt[j], term)
            if j < NX - 1:
                value = link[j + 1] * value
        lout[:, at] = value
        value = jnp.zeros((N, T), F32)
        for j in range(NX - 1, -1, -1):
            term = (cg[j, :, at].astype(F32) * wst[j, :, at]).astype(BF16)
            cs[j, :, at] = term
            rst[j, :, at] = value
            value = prow[j, :, at] * value + dot(rt[j], term)
            if j > 0:
                value = link[j] * value
        bout_l[:, at] = value

    def forward_copy(p):
        device = (lax.rem(c + NX, CTX), h)
        return remote(cout.at[p], cin.at[:, lanes(p, T)], cf_ss.at[p], cf_rs.at[p], device)

    def backward_copy(p):
        device = (lax.rem(c + CTX - NX, CTX), h)
        return remote(bout.at[p], bin_.at[:, lanes(p, T)], cb_ss.at[p], cb_rs.at[p], device)

    def forward_send(p):
        at = lanes(p, T)
        value = lout[:, at] + drow[NX, :, at] * cin[:, at].astype(F32)
        cout[p] = value.astype(BF16)
        forward_copy(p).start()

    def backward_send(p):
        at = lanes(p, T)
        value = bout_l[:, at] + erow[NX, :, at] * bin_[:, at].astype(F32)
        bout[p] = value.astype(BF16)
        backward_copy(p).start()

    def piece_copy(p, d, mine, theirs, send, recv):
        j = lax.rem(x + d, NX)
        k = p * NX + d
        return remote(mine.at[p, j], theirs.at[p, x], send.at[k], recv.at[k], (y * NX + j, h))

    def shared_copy(d, mine, theirs, k):
        e = lax.rem(h + d, HEADS)
        k = 2 * d + k
        return remote(mine.at[e], theirs.at[h], z_ss.at[k], z_rs.at[k], (c, e))

    def piece(p, local, scale, carried, proj, weight, terms, acc, mine, theirs, send, recv):
        at = lanes(p, T)
        value = carried[:, at].astype(F32)
        for d in (1, 3, 2, 0):
            j = lax.rem(x + d, NX)
            state = (local[j, :, at] + scale[j, :, at] * value).astype(BF16)
            out = (dot(proj[j], state) * weight[j, :, at]).astype(BF16)
            if d:
                mine[p, j] = out
                piece_copy(p, d, mine, theirs, send, recv).start()
            else:
                theirs[p, x] = out
            acc[j] += dot(terms[j, :, at], state, NT)

    def share_out(acc, first_lane, mine, theirs, k):
        acc[x] += gbl[:, first_lane : first_lane + N]
        for j in range(NX):
            mine[:, j, :, :] = acc[j].astype(BF16).reshape(HEADS, T // HEADS, N)

        def send(d, carry):
            shared_copy(d, mine, theirs, k).start()
            return carry

        lax.fori_loop(1, HEADS, send, 0)
        theirs[h] = mine[h]

    early = [
        pltpu.make_async_copy(ao_ref, ao_hbm, in_sem.at[0]),
        pltpu.make_async_copy(gq_ref, gq_hbm, in_sem.at[1]),
    ]

    def mixed(step, carry):
        pf = step - y
        pb = step - (NX - 1 - y)
        has_f = (pf >= 0) & (pf < 4)
        has_b = (pb >= 0) & (pb < 4)

        @pl.when(step < 4)
        def _():
            block_sums(step)

        @pl.when(has_f & (y > 0))
        def _():
            forward_copy(pf).wait_recv()

        @pl.when(has_f & (y < NX - 1))
        def _():
            forward_send(pf)

        @pl.when(has_b & (y < NX - 1))
        def _():
            backward_copy(pb).wait_recv()

        @pl.when(has_b & (y > 0))
        def _():
            backward_send(pb)

        @pl.when(has_f)
        def _():
            piece(pf, lst, drow, cin, rg, wst, cs, gc_acc, so_s, so_r, of_ss, of_rs)

        @pl.when(has_b)
        def _():
            piece(pb, rst, erow, bin_, bg, wen, xe, gb_acc, gx_s, gx_r, ob_ss, ob_rs)

        @pl.when(pf == 3)
        def _():
            share_out(gc_acc, N, gc_s, gc_r, 1)

        @pl.when(pb == 3)
        def _():
            share_out(gb_acc, 0, gb_s, gb_r, 0)

        @pl.when(step == 0)
        def _():
            lax.fori_loop(1, WIN, kv_wait, 0)
            lax.fori_loop(0, WIN, turned_block, 0)

        @pl.when(step < QL // 2)
        def _():
            head_pair(step, 0)

        @pl.when(step == 4)
        def _():
            for copy in early:
                copy.start()
            lax.fori_loop(1, 5, grads_block, 0)

        @pl.when(step == 5)
        def _():
            lax.fori_loop(5, WIN, grads_block, 0)
            own = slice(0, T)
            dkv_own[:, 0:T] = dot(dsall[own, :], qs[...]) * SCALE
            dkv_own[:, T : 2 * T] = dot(pall[own, :], dos[...])
            for d in (1, 3, 2):
                for copy in row_grads(d):
                    copy.start()

        return carry

    lax.fori_loop(0, NX - 1 + 4, mixed, 0)

    above = dkv_s[NX].astype(F32)
    up_sum[...] = dkv_s[2 * NX].astype(F32)
    for d in (1, 3, 2):
        for copy in row_grads(d):
            copy.wait_recv()
        above = above + dkv_r[2 * d].astype(F32)
        other = dkv_r[2 * d + 1].astype(F32)

        @pl.when(x < d)
        def _():
            dkv_own[...] += other

        @pl.when(x >= d)
        def _():
            up_sum[...] += other

    up_s[1] = above.astype(BF16)
    up_s[2] = up_sum[...].astype(BF16)
    for r in (1, 2):

        @pl.when(y >= r)
        def _():
            column_grads(r).start()

    def pieces_wait(p, carry):
        for d in (1, 3, 2):
            piece_copy(p, d, so_s, so_r, of_ss, of_rs).wait_recv()
            piece_copy(p, d, gx_s, gx_r, ob_ss, ob_rs).wait_recv()
        for s in range(NX):
            at = lanes(s * 4 + p, T)
            so_ref[:, at] = (lo[:, at] + so_r[p, s].astype(F32)).astype(BF16)
            gx_ref[:, at] = (lgx[:, at] + gx_r[p, s].astype(F32)).astype(BF16)
        return carry

    lax.fori_loop(0, 4, pieces_wait, 0)

    def shared_wait(d, carry):
        shared_copy(d, gb_s, gb_r, 0).wait_recv()
        shared_copy(d, gc_s, gc_r, 1).wait_recv()
        return carry

    lax.fori_loop(1, HEADS, shared_wait, 0)
    for k, ref in enumerate((gb_r, gc_r)):
        merged = ref[0].astype(F32)
        for e in range(1, HEADS):
            merged = merged + ref[e].astype(F32)
        gsum[:, k] = merged.astype(BF16)

    def owner_copy(d):
        j = lax.rem(x + d, NX)
        return remote(gsum.at[j], gr.at[x], gg_ss.at[d], gg_rs.at[d], (y * NX + j, h))

    for d in (1, 3, 2):
        owner_copy(d).start()
    gr[x] = gsum[x]

    for r in (1, 2):

        @pl.when(y + r < NX)
        def _():
            column_grads(r).wait_recv()
            dkv_own[...] += up_r[r].astype(F32)

    gk_ref[...] = dkv_own[:, 0:T].astype(BF16)
    gv_ref[...] = dkv_own[:, T : 2 * T].astype(BF16)

    for d in (1, 3, 2):
        owner_copy(d).wait_recv()
    owned = gr[0].astype(F32)
    for e in range(1, NX):
        owned = owned + gr[e].astype(F32)
    gb_ref[...] = owned[0].astype(BF16)
    gc_ref[...] = owned[1].astype(BF16)

    for r in (1, 2):

        @pl.when(y >= r)
        def _():
            column_grads(r).wait_send()

    for copy in early:
        copy.wait()

    def doc_done(d, carry):
        doc_copy(d).wait_send()
        return carry

    def kv_done(o, carry):
        @pl.when(c + o < CTX)
        def _():
            for copy in kv_copies(o):
                copy.wait_send()

        return carry

    def pieces_done(p, carry):
        for d in (1, 3, 2):
            for copy in token_copies(p, d):
                copy.wait_send()
            piece_copy(p, d, so_s, so_r, of_ss, of_rs).wait_send()
            piece_copy(p, d, gx_s, gx_r, ob_ss, ob_rs).wait_send()
        return carry

    def share_done(d, carry):
        for copy in share_copies(d):
            copy.wait_send()
        return carry

    def shared_done(d, carry):
        shared_copy(d, gb_s, gb_r, 0).wait_send()
        shared_copy(d, gc_s, gc_r, 1).wait_send()
        return carry

    def chain_done(p, carry):
        @pl.when(y < NX - 1)
        def _():
            forward_copy(p).wait_send()

        @pl.when(y > 0)
        def _():
            backward_copy(p).wait_send()

        return carry

    lax.fori_loop(1, CTX, doc_done, 0)
    lax.fori_loop(1, WIN, kv_done, 0)
    lax.fori_loop(0, 4, chain_done, 0)
    lax.fori_loop(0, 4, pieces_done, 0)
    lax.fori_loop(1, HEADS, share_done, 0)
    for d in (1, 3, 2):
        owner_copy(d).wait_send()
        decays[d].wait_send()
        for copy in slabs[d] + row_grads(d):
            copy.wait_send()
    lax.fori_loop(1, HEADS, shared_done, 0)


def body(q, k, v, do, doc, xs, b, cr, ld, ct):
    vm = pltpu.VMEM
    dma = pltpu.SemaphoreType.DMA
    scratch = [
        vm((T, QL * T), BF16),
        vm((T, QL * T), BF16),
        vm((T, QL * T), BF16),
        vm((T, QL * T), BF16),
        vm((T, NG * GL), BF16),
        vm((T, N), BF16),
        vm((T, N), BF16),
        vm((T, NG * GL), BF16),
        vm((KEYS, T), BF16),
        vm((KEYS, T), BF16),
        vm((T, KEYS), BF16),
        vm((T, KEYS), BF16),
        vm((CTX, 1, T), jnp.int32),
        vm((KEYS, 2 * T), F32),
        vm((QL * T, T), BF16),
        vm((QL * T, T), BF16),
        vm((KEYS, QL * T), BF16),
        vm((KEYS, QL * T), BF16),
        vm((T, 2 * T), F32),
        vm((WIN, T, 2 * T), BF16),
        vm((8, T, 2 * T), BF16),
        vm((T, 2 * T), F32),
        vm((3, T, 2 * T), BF16),
        vm((3, T, 2 * T), BF16),
        vm((NX, T, GL), BF16),
        vm((NX, T, GL), BF16),
        vm((NX, T, N), BF16),
        vm((NX, T, N), BF16),
        vm((32, T), F32),
        vm((NX, 8, T), F32),
        vm((NG, T, T), F32),
        vm((T, NG * GL), F32),
        vm((T, NG * GL), F32),
        vm((T, T), F32),
        vm((T, 2 * N), F32),
        vm((NX, T, GL), F32),
        vm((NX, T, GL), F32),
        vm((NX, T, GL), BF16),
        vm((NX, T, GL), BF16),
        vm((NX, N, T), BF16),
        vm((NX, N, T), BF16),
        vm((NX, N, GL), F32),
        vm((NX, N, GL), F32),
        vm((N, GL), F32),
        vm((N, GL), F32),
        vm((NX, 1, GL), F32),
        vm((NX + 1, 1, GL), F32),
        vm((NX + 1, 1, GL), F32),
        vm((N, GL), BF16),
        vm((4, N, T), BF16),
        vm((N, GL), BF16),
        vm((4, N, T), BF16),
        vm((4, NX, T, T), BF16),
        vm((4, NX, T, T), BF16),
        vm((4, NX, T, T), BF16),
        vm((4, NX, T, T), BF16),
        vm((NX, T, N), F32),
        vm((NX, T, N), F32),
        vm((HEADS, NX, T // HEADS, N), BF16),
        vm((HEADS, NX, T // HEADS, N), BF16),
        vm((HEADS, NX, T // HEADS, N), BF16),
        vm((HEADS, NX, T // HEADS, N), BF16),
        vm((NX, 2, T // HEADS, N), BF16),
        vm((NX, 2, T // HEADS, N), BF16),
        dma((8,)),
        dma((CTX,)),
        dma((CTX,)),
        dma((4,)),
        dma((4,)),
        dma((32,)),
        dma((32,)),
        dma((2 * WIN,)),
        dma((2 * WIN,)),
        dma((4,)),
        dma((4,)),
        dma((4,)),
        dma((4,)),
        dma((8,)),
        dma((8,)),
        dma((16,)),
        dma((16,)),
        dma((16,)),
        dma((16,)),
        dma((16,)),
        dma((16,)),
        dma((4,)),
        dma((4,)),
        dma((8,)),
        dma((8,)),
        dma((3,)),
        dma((3,)),
        dma((16,)),
        dma((16,)),
    ]
    shape = jax.ShapeDtypeStruct
    outs = (
        shape((T, QL * T), BF16),
        shape((T, NG * GL), BF16),
        shape((T, QL * T), BF16),
        shape((T, T), BF16),
        shape((T, T), BF16),
        shape((T, NG * GL), BF16),
        shape((T // HEADS, N), BF16),
        shape((T // HEADS, N), BF16),
    )
    here = pl.BlockSpec(memory_space=pltpu.VMEM)
    there = pl.BlockSpec(memory_space=pl.ANY)
    results = pl.pallas_call(
        kernel,
        name="packed_layers",
        out_shape=outs,
        in_specs=[there] * 4 + [here] + [there] * 3 + [here, there],
        out_specs=[there, here, there] + [here] * 5,
        scratch_shapes=scratch,
        compiler_params=pltpu.CompilerParams(
            collective_id=0, has_side_effects=True, vmem_limit_bytes=63 * 1024 * 1024
        ),
    )(q, k, v, do, doc.reshape(1, T), xs, b, cr, ld.T, ct)
    return pl.pallas_call(
        store,
        name="store_results",
        out_shape=outs,
        in_specs=[there] * 8,
        out_specs=[there] * 8,
        scratch_shapes=[pltpu.VMEM(out.shape, BF16) for out in outs] + [pltpu.SemaphoreType.DMA((16,))],
        compiler_params=pltpu.CompilerParams(vmem_limit_bytes=63 * 1024 * 1024),
    )(*results)


def store(*refs):
    sems = refs[24]
    copies = [
        (
            pltpu.make_async_copy(src, mid, sems.at[2 * i]),
            pltpu.make_async_copy(mid, dst, sems.at[2 * i + 1]),
        )
        for i, (src, dst, mid) in enumerate(zip(refs[:8], refs[8:16], refs[16:24]))
    ]
    for first, _ in copies:
        first.start()
    for first, second in copies:
        first.wait()
        second.start()
    for _, second in copies:
        second.wait()


def solution(mesh):
    both = P("ctx", "head")
    tokens = P("ctx", None)
    shared = P(("ctx", "head"), None)
    return jax.shard_map(
        body,
        mesh=mesh,
        in_specs=(both, both, both, both, P("ctx"), both, tokens, tokens, both, both),
        out_specs=(both, both, both, both, both, both, shared, shared),
        check_vma=False,
    )
```

```python
import jax
import jax.numpy as jnp
from jax import lax
from jax.experimental import pallas as pl
from jax.experimental.pallas import tpu as pltpu
from jax.sharding import PartitionSpec as P

MESH = pl.DeviceIdType.MESH
F32 = jnp.float32
BF16 = jnp.bfloat16
NEG = -1.0e30
SCALE = 128.0**-0.5

T = 128
CTX = 16
NX = 4
HEADS = 8
QL = 8
WIN = 9
KEYS = WIN * T
N = 256
GL = 512
NG = 4

NN = (((1,), (0,)), ((), ()))
NT = (((1,), (1,)), ((), ()))
TN = (((0,), (0,)), ((), ()))


def dot(a, b, dims=NN):
    return lax.dot_general(a, b, dims, preferred_element_type=F32)


def remote(src, dst, send, recv, device):
    return pltpu.make_async_remote_copy(
        src_ref=src,
        dst_ref=dst,
        send_sem=send,
        recv_sem=recv,
        device_id=device,
        device_id_type=MESH,
    )


def lanes(i, width):
    return pl.ds(pl.multiple_of(i * width, width), width)


def column_of(row):
    return jnp.broadcast_to(row, (T, T)).T


def kernel(
    q_hbm,
    k_hbm,
    v_hbm,
    do_hbm,
    doc_ref,
    x_hbm,
    b_hbm,
    c_hbm,
    ld_ref,
    ct_hbm,
    ao_hbm,
    so_ref,
    gq_hbm,
    gk_ref,
    gv_ref,
    gx_ref,
    gb_ref,
    gc_ref,
    ao_ref,
    gq_ref,
    q_ref,
    do_ref,
    x_ref,
    b_ref,
    c_ref,
    ct_ref,
    kwin,
    vwin,
    kt,
    vt,
    docs,
    bias,
    qs,
    dos,
    pall,
    dsall,
    dkv_own,
    dkv_s,
    dkv_r,
    up_sum,
    up_s,
    up_r,
    xg,
    cg,
    bg,
    rg,
    cumr,
    dg,
    ccol,
    lo,
    lgx,
    wsum,
    gbl,
    wst,
    wen,
    xe,
    cs,
    bt,
    rt,
    lst,
    rst,
    lout,
    bout_l,
    prow,
    drow,
    erow,
    cin,
    cout,
    bin_,
    bout,
    so_s,
    gx_s,
    so_r,
    gx_r,
    gb_acc,
    gc_acc,
    gb_s,
    gc_s,
    gb_r,
    gc_r,
    gsum,
    gr,
    in_sem,
    doc_ss,
    doc_rs,
    dc_ss,
    dc_rs,
    xa_ss,
    xa_rs,
    kv_ss,
    kv_rs,
    cf_ss,
    cf_rs,
    cb_ss,
    cb_rs,
    bc_ss,
    bc_rs,
    hd_ss,
    hd_rs,
    of_ss,
    of_rs,
    ob_ss,
    ob_rs,
    gg_ss,
    gg_rs,
    dkv_ss,
    dkv_rs,
    up_ss,
    up_rs,
    z_ss,
    z_rs,
):
    c = lax.axis_index("ctx")
    h = lax.axis_index("head")
    y = c // NX
    x = lax.rem(c, NX)

    def ctx_at(d):
        return (lax.rem(c + d + CTX, CTX), h)

    def row_at(d):
        return y * NX + lax.rem(x + d, NX)

    barrier = pltpu.get_barrier_semaphore()

    def greet_ctx(d, carry):
        pl.semaphore_signal(barrier, inc=1, device_id=ctx_at(d), device_id_type=MESH)
        return carry

    def greet_head(d, carry):
        pl.semaphore_signal(
            barrier, inc=1, device_id=(c, lax.rem(h + d, HEADS)), device_id_type=MESH
        )
        return carry

    lax.fori_loop(1, CTX, greet_ctx, 0)
    lax.fori_loop(1, HEADS, greet_head, 0)

    own_rows = pl.ds(0, T)
    loads = [
        pltpu.make_async_copy(src, dst, in_sem.at[i])
        for i, (src, dst) in enumerate(
            (
                (b_hbm, b_ref),
                (c_hbm, c_ref),
                (x_hbm, x_ref),
                (ct_hbm, ct_ref),
                (k_hbm, kwin.at[own_rows]),
                (v_hbm, vwin.at[own_rows]),
                (q_hbm, q_ref),
                (do_hbm, do_ref),
            )
        )
    ]
    for load in loads:
        load.start()

    row_i = lax.broadcasted_iota(jnp.int32, (T, T), 0)
    col_i = lax.broadcasted_iota(jnp.int32, (T, T), 1)
    upto = (row_i <= col_i).astype(F32)
    low_half = col_i < 64

    cumr[...] = lax.dot_general(
        ld_ref[...], upto, NN, precision=lax.Precision.HIGHEST, preferred_element_type=F32
    )
    my_slab = pl.ds(pl.multiple_of(h * 16, 16), 16)

    pl.semaphore_wait(barrier, CTX - 1 + HEADS - 1)

    def doc_copy(d):
        return remote(doc_ref, docs.at[c], doc_ss.at[d], doc_rs.at[d], ctx_at(d))

    def doc_send(d, carry):
        doc_copy(d).start()
        return carry

    def slab_copies(d):
        device = (row_at(d), h)
        pairs = ((b_hbm, bg), (c_hbm, rg))
        return [
            remote(
                src.at[my_slab],
                dst.at[x, my_slab],
                bc_ss.at[d * 2 + i],
                bc_rs.at[d * 2 + i],
                device,
            )
            for i, (src, dst) in enumerate(pairs)
        ]

    def share_copies(d):
        device = (c, lax.rem(h + d, HEADS))
        return [
            remote(
                ref.at[:, my_slab, :],
                ref.at[:, my_slab, :],
                hd_ss.at[d * 2 + i],
                hd_rs.at[d * 2 + i],
                device,
            )
            for i, ref in enumerate((bg, rg))
        ]

    def decay_copy(d):
        t = lax.rem(x + d, NX)
        rows = cumr.at[pl.ds(pl.multiple_of(t * 8, 8), 8)]
        return remote(rows, dg.at[x], dc_ss.at[d], dc_rs.at[d], (y * NX + t, h))

    def token_copies(p, d):
        t = lax.rem(x + d, NX)
        src = lanes(t * 4 + p, T)
        dst = lanes(p, T)
        k = (p * NX + d) * 2
        return [
            remote(
                ref.at[:, src],
                out.at[x, :, dst],
                xa_ss.at[k + i],
                xa_rs.at[k + i],
                (y * NX + t, h),
            )
            for i, (ref, out) in enumerate(((x_hbm, xg), (ct_hbm, cg)))
        ]

    slabs = {d: slab_copies(d) for d in (1, 3, 2)}
    decays = {d: decay_copy(d) for d in (1, 3, 2)}
    for d in (1, 3, 2):
        for copy in slabs[d]:
            copy.start()
        decays[d].start()
    lax.fori_loop(1, CTX, doc_send, 0)

    def kv_copies(o):
        rows = pl.ds(pl.multiple_of(o * T, T), T)
        return (
            remote(k_hbm, kwin.at[rows], kv_ss.at[2 * o], kv_rs.at[2 * o], ctx_at(o)),
            remote(v_hbm, vwin.at[rows], kv_ss.at[2 * o + 1], kv_rs.at[2 * o + 1], ctx_at(o)),
        )

    def kv_send(o, carry):
        @pl.when(c + o < CTX)
        def _():
            for copy in kv_copies(o):
                copy.start()

        @pl.when(c < o)
        def _():
            rows = pl.ds(pl.multiple_of(o * T, T), T)
            kwin[rows, :] = jnp.zeros((T, T), BF16)
            vwin[rows, :] = jnp.zeros((T, T), BF16)

        return carry

    lax.fori_loop(1, WIN, kv_send, 0)

    def token_send(p, carry):
        for d in (1, 3, 2):
            for copy in token_copies(p, d):
                copy.start()
        return carry

    lax.fori_loop(0, 4, token_send, 0)

    for load in loads:
        load.wait()
    docs[c] = doc_ref[...]
    xg[x] = x_ref[:, lanes(x, GL)]
    cg[x] = ct_ref[:, lanes(x, GL)]
    bg[x, my_slab, :] = b_ref[my_slab, :]
    rg[x, my_slab, :] = c_ref[my_slab, :]
    dg[x] = cumr[pl.ds(pl.multiple_of(x * 8, 8), 8), :]

    for d in (1, 3, 2):
        for copy in slabs[d]:
            copy.wait_recv()

    def share(d, carry):
        for copy in share_copies(d):
            copy.start()
        return carry

    lax.fori_loop(1, HEADS, share, 0)

    doc_row = doc_ref[...].astype(F32)
    doc_col = column_of(doc_row)
    local_bias = jnp.where((doc_row == doc_col) & (col_i <= row_i), 0.0, NEG)
    gram = dot(c_ref[...], b_ref[...], NT)
    wsum[...] = jnp.zeros((T, T), F32)

    def columns(g, carry):
        rows = cumr[pl.ds(pl.multiple_of(g * 8, 8), 8), :]
        ccol[g] = jnp.concatenate([rows, jnp.zeros((T - 8, T), F32)], axis=0).T
        return carry

    lax.fori_loop(0, NG, columns, 0)
    half_mask = low_half.astype(BF16)
    other_mask = (~low_half).astype(BF16)

    def local_group(g, carry):
        rows = cumr[pl.ds(pl.multiple_of(g * 8, 8), 8), :]
        cols = ccol[g]
        total = wsum[...]
        for p in range(4):
            at = lanes(g * 4 + p, T)
            xp = x_ref[:, at]
            cp = ct_ref[:, at]
            x2 = jnp.concatenate([xp * half_mask, xp * other_mask], axis=0)
            c2 = jnp.concatenate([cp * half_mask, cp * other_mask], axis=0)
            inner = dot(c2, xp, NT)
            mix = []
            for i in range(2):
                j = 2 * p + i
                decay = jnp.exp(cols[:, j : j + 1] - rows[j : j + 1, :] + local_bias)
                mix.append((decay * gram).astype(BF16))
                total = total + decay * inner[i * T : (i + 1) * T]
            lo[:, at] = dot(jnp.concatenate(mix, axis=1), x2)
            lgx[:, at] = dot(jnp.concatenate(mix, axis=0), c2, TN)
        wsum[...] = total
        return carry

    lax.fori_loop(0, NG, local_group, 0)
    weighted = wsum[...].astype(BF16)
    gbl[:, 0:N] = dot(weighted, c_ref[...], TN)
    gbl[:, N : 2 * N] = dot(weighted, b_ref[...])

    def doc_wait(d, carry):
        doc_copy(d).wait_recv()
        return carry

    lax.fori_loop(1, CTX, doc_wait, 0)
    for d in (1, 3, 2):
        decays[d].wait_recv()

    def bias_block(o, carry):
        rows = pl.ds(pl.multiple_of(o * T, T), T)
        kb = lax.rem(c - o + CTX, CTX)
        key_doc = column_of(docs[kb].astype(F32))
        allowed = (key_doc == doc_row) & (kb * T + row_i <= c * T + col_i)
        block = jnp.where(allowed, 0.0, NEG)
        bias[rows, 0:T] = block
        bias[rows, T : 2 * T] = block
        return carry

    def stack_head(i, carry):
        rows = pl.ds(pl.multiple_of(i * T, T), T)
        qs[rows, :] = q_ref[:, lanes(i, T)]
        dos[rows, :] = do_ref[:, lanes(i, T)]
        return carry

    lax.fori_loop(0, WIN, bias_block, 0)
    lax.fori_loop(0, QL, stack_head, 0)

    def weights_of(j, carry):
        cum = dg[j]
        docj = docs[y * NX + j].astype(F32)
        start = jnp.where(docj == docj[:, 0:1], 1.0, 0.0)
        end = jnp.where(docj == docj[:, T - 1 : T], 1.0, 0.0)
        w_start = jnp.exp(cum) * start
        w_end = jnp.exp(cum[:, T - 1 : T] - cum) * end
        table = jnp.concatenate([w_start, w_end, jnp.zeros((T - 16, T), F32)], axis=0).T
        for p in range(4):
            at = slice(p * T, (p + 1) * T)
            ws = jnp.where(low_half, table[:, 2 * p : 2 * p + 1], table[:, 2 * p + 1 : 2 * p + 2])
            we = jnp.where(
                low_half, table[:, 8 + 2 * p : 9 + 2 * p], table[:, 9 + 2 * p : 10 + 2 * p]
            )
            wst[j, :, at] = ws
            wen[j, :, at] = we
            prow[j, :, at] = ws[T - 1 : T, :]
        return carry

    lax.fori_loop(0, NX, weights_of, 0)

    def edge(j, side):
        at = 0 if side == 0 else T - 1
        return docs[j].astype(F32)[:, at : at + 1]

    def linked(first, last, inside):
        same = edge(first, 0) == edge(last, 1)
        return jnp.where(same & inside, 1.0, 0.0)

    base = y * NX
    link = [linked(base, jnp.maximum(base - 1, 0), y > 0)]
    link += [linked(base + j, base + j - 1, y >= 0) for j in range(1, NX)]
    link += [linked(jnp.minimum(base + NX, CTX - 1), base + NX - 1, y < NX - 1)]
    wide = [jnp.broadcast_to(value, (1, GL)) for value in link]

    drow[0] = wide[0]
    for j in range(NX - 1):
        drow[j + 1] = wide[j + 1] * prow[j] * drow[j]
    drow[NX] = prow[NX - 1] * drow[NX - 1]
    erow[NX - 1] = wide[NX]
    for j in range(NX - 1, 0, -1):
        erow[j - 1] = wide[j] * prow[j] * erow[j]
    erow[NX] = prow[0] * erow[0]

    @pl.when(y == 0)
    def _():
        cin[...] = jnp.zeros((N, GL), BF16)

    @pl.when(y == NX - 1)
    def _():
        bin_[...] = jnp.zeros((N, GL), BF16)

    def kv_wait(o, carry):
        @pl.when(c >= o)
        def _():
            for copy in kv_copies(o):
                copy.wait_recv()

        return carry

    def turned_block(o, carry):
        rows = pl.ds(pl.multiple_of(o * T, T), T)
        kt[:, rows] = kwin[rows, :].T
        vt[:, rows] = vwin[rows, :].T
        return carry

    def head_pair(i, carry):
        two = 2 * T
        at = lanes(i, two)
        rows = pl.ds(pl.multiple_of(i * two, two), two)
        first = lanes(2 * i, T)
        second = lanes(2 * i + 1, T)
        q2 = qs[rows, :]
        do2 = dos[rows, :]
        scores = dot(kwin[...], q2, NT) * SCALE + bias[...]
        top = jnp.max(scores, axis=0, keepdims=True)
        weights = jnp.exp(scores - top)
        total = jnp.sum(weights, axis=0, keepdims=True)
        out_t = dot(vt[...], weights.astype(BF16)) / total
        out = out_t.T.astype(BF16)
        ao_ref[:, first] = out[:T]
        ao_ref[:, second] = out[T:]
        low = out_t.astype(BF16).astype(F32)
        inner = jnp.sum(low * do2.astype(F32).T, axis=0, keepdims=True)
        prob = weights * (1.0 / total)
        dscore = (prob * (dot(vwin[...], do2, NT) - inner)).astype(BF16)
        pall[:, at] = prob.astype(BF16)
        dsall[:, at] = dscore
        gq = (dot(kt[...], dscore) * SCALE).T.astype(BF16)
        gq_ref[:, first] = gq[:T]
        gq_ref[:, second] = gq[T:]
        return carry

    def row_grads(d):
        t = lax.rem(x + d, NX)
        device = (y * NX + t, h)
        blocks = (NX + x - t, lax.rem(2 * NX + x - t, 2 * NX))
        return [
            remote(
                dkv_s.at[o],
                dkv_r.at[2 * d + i],
                dkv_ss.at[2 * d + i],
                dkv_rs.at[2 * d + i],
                device,
            )
            for i, o in enumerate(blocks)
        ]

    def column_grads(r):
        device = (lax.rem(c + CTX - r * NX, CTX), h)
        return remote(up_s.at[r], up_r.at[r], up_ss.at[r], up_rs.at[r], device)

    def grads_block(o, carry):
        rows = pl.ds(pl.multiple_of(o * T, T), T)
        dkv_s[o, :, 0:T] = (dot(dsall[rows, :], qs[...]) * SCALE).astype(BF16)
        dkv_s[o, :, T : 2 * T] = dot(pall[rows, :], dos[...]).astype(BF16)
        return carry

    def share_wait(d, carry):
        for copy in share_copies(d):
            copy.wait_recv()
        return carry

    lax.fori_loop(1, HEADS, share_wait, 0)
    for j in range(NX):
        bt[j] = bg[j].T
        rt[j] = rg[j].T
        gc_acc[j] = jnp.zeros((T, N), F32)
        gb_acc[j] = jnp.zeros((T, N), F32)

    def block_sums(p):
        at = lanes(p, T)
        for d in (1, 3, 2):
            for copy in token_copies(p, d):
                copy.wait_recv()
        value = jnp.zeros((N, T), F32)
        for j in range(NX):
            term = (xg[j, :, at].astype(F32) * wen[j, :, at]).astype(BF16)
            xe[j, :, at] = term
            lst[j, :, at] = value
            value = prow[j, :, at] * value + dot(bt[j], term)
            if j < NX - 1:
                value = link[j + 1] * value
        lout[:, at] = value
        value = jnp.zeros((N, T), F32)
        for j in range(NX - 1, -1, -1):
            term = (cg[j, :, at].astype(F32) * wst[j, :, at]).astype(BF16)
            cs[j, :, at] = term
            rst[j, :, at] = value
            value = prow[j, :, at] * value + dot(rt[j], term)
            if j > 0:
                value = link[j] * value
        bout_l[:, at] = value

    def forward_copy(p):
        device = (lax.rem(c + NX, CTX), h)
        return remote(cout.at[p], cin.at[:, lanes(p, T)], cf_ss.at[p], cf_rs.at[p], device)

    def backward_copy(p):
        device = (lax.rem(c + CTX - NX, CTX), h)
        return remote(bout.at[p], bin_.at[:, lanes(p, T)], cb_ss.at[p], cb_rs.at[p], device)

    def forward_send(p):
        at = lanes(p, T)
        value = lout[:, at] + drow[NX, :, at] * cin[:, at].astype(F32)
        cout[p] = value.astype(BF16)
        forward_copy(p).start()

    def backward_send(p):
        at = lanes(p, T)
        value = bout_l[:, at] + erow[NX, :, at] * bin_[:, at].astype(F32)
        bout[p] = value.astype(BF16)
        backward_copy(p).start()

    def piece_copy(p, d, mine, theirs, send, recv):
        j = lax.rem(x + d, NX)
        k = p * NX + d
        return remote(mine.at[p, j], theirs.at[p, x], send.at[k], recv.at[k], (y * NX + j, h))

    def shared_copy(d, mine, theirs, k):
        e = lax.rem(h + d, HEADS)
        k = 2 * d + k
        return remote(mine.at[e], theirs.at[h], z_ss.at[k], z_rs.at[k], (c, e))

    def piece(p, local, scale, carried, proj, weight, terms, acc, mine, theirs, send, recv):
        at = lanes(p, T)
        value = carried[:, at].astype(F32)
        for d in (1, 3, 2, 0):
            j = lax.rem(x + d, NX)
            state = (local[j, :, at] + scale[j, :, at] * value).astype(BF16)
            out = (dot(proj[j], state) * weight[j, :, at]).astype(BF16)
            if d:
                mine[p, j] = out
                piece_copy(p, d, mine, theirs, send, recv).start()
            else:
                theirs[p, x] = out
            acc[j] += dot(terms[j, :, at], state, NT)

    def share_out(acc, first_lane, mine, theirs, k):
        acc[x] += gbl[:, first_lane : first_lane + N]
        for j in range(NX):
            mine[:, j, :, :] = acc[j].astype(BF16).reshape(HEADS, T // HEADS, N)

        def send(d, carry):
            shared_copy(d, mine, theirs, k).start()
            return carry

        lax.fori_loop(1, HEADS, send, 0)
        theirs[h] = mine[h]

    early = [
        pltpu.make_async_copy(ao_ref, ao_hbm, in_sem.at[0]),
        pltpu.make_async_copy(gq_ref, gq_hbm, in_sem.at[1]),
    ]

    def mixed(step, carry):
        pf = step - y
        pb = step - (NX - 1 - y)
        has_f = (pf >= 0) & (pf < 4)
        has_b = (pb >= 0) & (pb < 4)

        @pl.when(step < 4)
        def _():
            block_sums(step)

        @pl.when(has_f & (y > 0))
        def _():
            forward_copy(pf).wait_recv()

        @pl.when(has_f & (y < NX - 1))
        def _():
            forward_send(pf)

        @pl.when(has_b & (y < NX - 1))
        def _():
            backward_copy(pb).wait_recv()

        @pl.when(has_b & (y > 0))
        def _():
            backward_send(pb)

        @pl.when(has_f)
        def _():
            piece(pf, lst, drow, cin, rg, wst, cs, gc_acc, so_s, so_r, of_ss, of_rs)

        @pl.when(has_b)
        def _():
            piece(pb, rst, erow, bin_, bg, wen, xe, gb_acc, gx_s, gx_r, ob_ss, ob_rs)

        @pl.when(pf == 3)
        def _():
            share_out(gc_acc, N, gc_s, gc_r, 1)

        @pl.when(pb == 3)
        def _():
            share_out(gb_acc, 0, gb_s, gb_r, 0)

        @pl.when(step == 0)
        def _():
            lax.fori_loop(1, WIN, kv_wait, 0)
            lax.fori_loop(0, WIN, turned_block, 0)

        @pl.when(step < QL // 2)
        def _():
            head_pair(step, 0)

        @pl.when(step == 4)
        def _():
            for copy in early:
                copy.start()
            lax.fori_loop(1, WIN, grads_block, 0)
            for d in (1, 3, 2):
                for copy in row_grads(d):
                    copy.start()

        @pl.when(step == 5)
        def _():
            own = slice(0, T)
            dkv_own[:, 0:T] = dot(dsall[own, :], qs[...]) * SCALE
            dkv_own[:, T : 2 * T] = dot(pall[own, :], dos[...])

        return carry

    lax.fori_loop(0, NX - 1 + 4, mixed, 0)

    above = dkv_s[NX].astype(F32)
    up_sum[...] = dkv_s[2 * NX].astype(F32)
    for d in (1, 3, 2):
        for copy in row_grads(d):
            copy.wait_recv()
        above = above + dkv_r[2 * d].astype(F32)
        other = dkv_r[2 * d + 1].astype(F32)

        @pl.when(x < d)
        def _():
            dkv_own[...] += other

        @pl.when(x >= d)
        def _():
            up_sum[...] += other

    up_s[1] = above.astype(BF16)
    up_s[2] = up_sum[...].astype(BF16)
    for r in (1, 2):

        @pl.when(y >= r)
        def _():
            column_grads(r).start()

    def pieces_wait(p, carry):
        for d in (1, 3, 2):
            piece_copy(p, d, so_s, so_r, of_ss, of_rs).wait_recv()
            piece_copy(p, d, gx_s, gx_r, ob_ss, ob_rs).wait_recv()
        for s in range(NX):
            at = lanes(s * 4 + p, T)
            so_ref[:, at] = (lo[:, at] + so_r[p, s].astype(F32)).astype(BF16)
            gx_ref[:, at] = (lgx[:, at] + gx_r[p, s].astype(F32)).astype(BF16)
        return carry

    lax.fori_loop(0, 4, pieces_wait, 0)

    def shared_wait(d, carry):
        shared_copy(d, gb_s, gb_r, 0).wait_recv()
        shared_copy(d, gc_s, gc_r, 1).wait_recv()
        return carry

    lax.fori_loop(1, HEADS, shared_wait, 0)
    for k, ref in enumerate((gb_r, gc_r)):
        merged = ref[0].astype(F32)
        for e in range(1, HEADS):
            merged = merged + ref[e].astype(F32)
        gsum[:, k] = merged.astype(BF16)

    def owner_copy(d):
        j = lax.rem(x + d, NX)
        return remote(gsum.at[j], gr.at[x], gg_ss.at[d], gg_rs.at[d], (y * NX + j, h))

    for d in (1, 3, 2):
        owner_copy(d).start()
    gr[x] = gsum[x]

    for r in (1, 2):

        @pl.when(y + r < NX)
        def _():
            column_grads(r).wait_recv()
            dkv_own[...] += up_r[r].astype(F32)

    gk_ref[...] = dkv_own[:, 0:T].astype(BF16)
    gv_ref[...] = dkv_own[:, T : 2 * T].astype(BF16)

    for d in (1, 3, 2):
        owner_copy(d).wait_recv()
    owned = gr[0].astype(F32)
    for e in range(1, NX):
        owned = owned + gr[e].astype(F32)
    gb_ref[...] = owned[0].astype(BF16)
    gc_ref[...] = owned[1].astype(BF16)

    for r in (1, 2):

        @pl.when(y >= r)
        def _():
            column_grads(r).wait_send()

    for copy in early:
        copy.wait()

    def doc_done(d, carry):
        doc_copy(d).wait_send()
        return carry

    def kv_done(o, carry):
        @pl.when(c + o < CTX)
        def _():
            for copy in kv_copies(o):
                copy.wait_send()

        return carry

    def pieces_done(p, carry):
        for d in (1, 3, 2):
            for copy in token_copies(p, d):
                copy.wait_send()
            piece_copy(p, d, so_s, so_r, of_ss, of_rs).wait_send()
            piece_copy(p, d, gx_s, gx_r, ob_ss, ob_rs).wait_send()
        return carry

    def share_done(d, carry):
        for copy in share_copies(d):
            copy.wait_send()
        return carry

    def shared_done(d, carry):
        shared_copy(d, gb_s, gb_r, 0).wait_send()
        shared_copy(d, gc_s, gc_r, 1).wait_send()
        return carry

    def chain_done(p, carry):
        @pl.when(y < NX - 1)
        def _():
            forward_copy(p).wait_send()

        @pl.when(y > 0)
        def _():
            backward_copy(p).wait_send()

        return carry

    lax.fori_loop(1, CTX, doc_done, 0)
    lax.fori_loop(1, WIN, kv_done, 0)
    lax.fori_loop(0, 4, chain_done, 0)
    lax.fori_loop(0, 4, pieces_done, 0)
    lax.fori_loop(1, HEADS, share_done, 0)
    for d in (1, 3, 2):
        owner_copy(d).wait_send()
        decays[d].wait_send()
        for copy in slabs[d] + row_grads(d):
            copy.wait_send()
    lax.fori_loop(1, HEADS, shared_done, 0)


def body(q, k, v, do, doc, xs, b, cr, ld, ct):
    vm = pltpu.VMEM
    dma = pltpu.SemaphoreType.DMA
    scratch = [
        vm((T, QL * T), BF16),
        vm((T, QL * T), BF16),
        vm((T, QL * T), BF16),
        vm((T, QL * T), BF16),
        vm((T, NG * GL), BF16),
        vm((T, N), BF16),
        vm((T, N), BF16),
        vm((T, NG * GL), BF16),
        vm((KEYS, T), BF16),
        vm((KEYS, T), BF16),
        vm((T, KEYS), BF16),
        vm((T, KEYS), BF16),
        vm((CTX, 1, T), jnp.int32),
        vm((KEYS, 2 * T), F32),
        vm((QL * T, T), BF16),
        vm((QL * T, T), BF16),
        vm((KEYS, QL * T), BF16),
        vm((KEYS, QL * T), BF16),
        vm((T, 2 * T), F32),
        vm((WIN, T, 2 * T), BF16),
        vm((8, T, 2 * T), BF16),
        vm((T, 2 * T), F32),
        vm((3, T, 2 * T), BF16),
        vm((3, T, 2 * T), BF16),
        vm((NX, T, GL), BF16),
        vm((NX, T, GL), BF16),
        vm((NX, T, N), BF16),
        vm((NX, T, N), BF16),
        vm((32, T), F32),
        vm((NX, 8, T), F32),
        vm((NG, T, T), F32),
        vm((T, NG * GL), F32),
        vm((T, NG * GL), F32),
        vm((T, T), F32),
        vm((T, 2 * N), F32),
        vm((NX, T, GL), F32),
        vm((NX, T, GL), F32),
        vm((NX, T, GL), BF16),
        vm((NX, T, GL), BF16),
        vm((NX, N, T), BF16),
        vm((NX, N, T), BF16),
        vm((NX, N, GL), F32),
        vm((NX, N, GL), F32),
        vm((N, GL), F32),
        vm((N, GL), F32),
        vm((NX, 1, GL), F32),
        vm((NX + 1, 1, GL), F32),
        vm((NX + 1, 1, GL), F32),
        vm((N, GL), BF16),
        vm((4, N, T), BF16),
        vm((N, GL), BF16),
        vm((4, N, T), BF16),
        vm((4, NX, T, T), BF16),
        vm((4, NX, T, T), BF16),
        vm((4, NX, T, T), BF16),
        vm((4, NX, T, T), BF16),
        vm((NX, T, N), F32),
        vm((NX, T, N), F32),
        vm((HEADS, NX, T // HEADS, N), BF16),
        vm((HEADS, NX, T // HEADS, N), BF16),
        vm((HEADS, NX, T // HEADS, N), BF16),
        vm((HEADS, NX, T // HEADS, N), BF16),
        vm((NX, 2, T // HEADS, N), BF16),
        vm((NX, 2, T // HEADS, N), BF16),
        dma((8,)),
        dma((CTX,)),
        dma((CTX,)),
        dma((4,)),
        dma((4,)),
        dma((32,)),
        dma((32,)),
        dma((2 * WIN,)),
        dma((2 * WIN,)),
        dma((4,)),
        dma((4,)),
        dma((4,)),
        dma((4,)),
        dma((8,)),
        dma((8,)),
        dma((16,)),
        dma((16,)),
        dma((16,)),
        dma((16,)),
        dma((16,)),
        dma((16,)),
        dma((4,)),
        dma((4,)),
        dma((8,)),
        dma((8,)),
        dma((3,)),
        dma((3,)),
        dma((16,)),
        dma((16,)),
    ]
    shape = jax.ShapeDtypeStruct
    outs = (
        shape((T, QL * T), BF16),
        shape((T, NG * GL), BF16),
        shape((T, QL * T), BF16),
        shape((T, T), BF16),
        shape((T, T), BF16),
        shape((T, NG * GL), BF16),
        shape((T // HEADS, N), BF16),
        shape((T // HEADS, N), BF16),
    )
    here = pl.BlockSpec(memory_space=pltpu.VMEM)
    there = pl.BlockSpec(memory_space=pl.ANY)
    results = pl.pallas_call(
        kernel,
        name="packed_layers",
        out_shape=outs,
        in_specs=[there] * 4 + [here] + [there] * 3 + [here, there],
        out_specs=[there, here, there] + [here] * 5,
        scratch_shapes=scratch,
        compiler_params=pltpu.CompilerParams(
            collective_id=0, has_side_effects=True, vmem_limit_bytes=63 * 1024 * 1024
        ),
    )(q, k, v, do, doc.reshape(1, T), xs, b, cr, ld.T, ct)
    return pl.pallas_call(
        store,
        name="store_results",
        out_shape=outs,
        in_specs=[there] * 8,
        out_specs=[there] * 8,
        scratch_shapes=[pltpu.VMEM(out.shape, BF16) for out in outs] + [pltpu.SemaphoreType.DMA((16,))],
        compiler_params=pltpu.CompilerParams(vmem_limit_bytes=63 * 1024 * 1024),
    )(*results)


def store(*refs):
    sems = refs[24]
    copies = [
        (
            pltpu.make_async_copy(src, mid, sems.at[2 * i]),
            pltpu.make_async_copy(mid, dst, sems.at[2 * i + 1]),
        )
        for i, (src, dst, mid) in enumerate(zip(refs[:8], refs[8:16], refs[16:24]))
    ]
    for first, _ in copies:
        first.start()
    for first, second in copies:
        first.wait()
        second.start()
    for _, second in copies:
        second.wait()


def solution(mesh):
    both = P("ctx", "head")
    tokens = P("ctx", None)
    shared = P(("ctx", "head"), None)
    return jax.shard_map(
        body,
        mesh=mesh,
        in_specs=(both, both, both, both, P("ctx"), both, tokens, tokens, both, both),
        out_specs=(both, both, both, both, both, both, shared, shared),
        check_vma=False,
    )
```

```python
import jax
import jax.numpy as jnp
from jax import lax
from jax.experimental import pallas as pl
from jax.experimental.pallas import tpu as pltpu
from jax.sharding import PartitionSpec as P

MESH = pl.DeviceIdType.MESH
F32 = jnp.float32
BF16 = jnp.bfloat16
NEG = -1.0e30
SCALE = 128.0**-0.5

T = 128
CTX = 16
NX = 4
HEADS = 8
QL = 8
WIN = 9
KEYS = WIN * T
N = 256
GL = 512
NG = 4

NN = (((1,), (0,)), ((), ()))
NT = (((1,), (1,)), ((), ()))
TN = (((0,), (0,)), ((), ()))


def dot(a, b, dims=NN):
    return lax.dot_general(a, b, dims, preferred_element_type=F32)


def remote(src, dst, send, recv, device):
    return pltpu.make_async_remote_copy(
        src_ref=src,
        dst_ref=dst,
        send_sem=send,
        recv_sem=recv,
        device_id=device,
        device_id_type=MESH,
    )


def lanes(i, width):
    return pl.ds(pl.multiple_of(i * width, width), width)


def column_of(row):
    return jnp.broadcast_to(row, (T, T)).T


def kernel(
    q_hbm,
    k_hbm,
    v_hbm,
    do_hbm,
    doc_ref,
    x_hbm,
    b_hbm,
    c_hbm,
    ld_ref,
    ct_hbm,
    ao_hbm,
    so_ref,
    gq_hbm,
    gk_ref,
    gv_ref,
    gx_ref,
    gb_ref,
    gc_ref,
    ao_ref,
    gq_ref,
    q_ref,
    do_ref,
    x_ref,
    b_ref,
    c_ref,
    ct_ref,
    kwin,
    vwin,
    kt,
    vt,
    docs,
    bias,
    qs,
    dos,
    pall,
    dsall,
    dkv_own,
    dkv_s,
    dkv_r,
    up_one,
    up_sum,
    up_s,
    up_r,
    xg,
    cg,
    bg,
    rg,
    cumr,
    dg,
    ccol,
    lo,
    lgx,
    wsum,
    gbl,
    wst,
    wen,
    xe,
    cs,
    bt,
    rt,
    lst,
    rst,
    lout,
    bout_l,
    prow,
    drow,
    erow,
    cin,
    cout,
    bin_,
    bout,
    so_s,
    gx_s,
    so_r,
    gx_r,
    gb_acc,
    gc_acc,
    gb_s,
    gc_s,
    gb_r,
    gc_r,
    gsum,
    gr,
    in_sem,
    doc_ss,
    doc_rs,
    dc_ss,
    dc_rs,
    xa_ss,
    xa_rs,
    kv_ss,
    kv_rs,
    cf_ss,
    cf_rs,
    cb_ss,
    cb_rs,
    bc_ss,
    bc_rs,
    hd_ss,
    hd_rs,
    of_ss,
    of_rs,
    ob_ss,
    ob_rs,
    gg_ss,
    gg_rs,
    dkv_ss,
    dkv_rs,
    up_ss,
    up_rs,
    z_ss,
    z_rs,
):
    c = lax.axis_index("ctx")
    h = lax.axis_index("head")
    y = c // NX
    x = lax.rem(c, NX)

    def ctx_at(d):
        return (lax.rem(c + d + CTX, CTX), h)

    def row_at(d):
        return y * NX + lax.rem(x + d, NX)

    barrier = pltpu.get_barrier_semaphore()

    def greet_ctx(d, carry):
        pl.semaphore_signal(barrier, inc=1, device_id=ctx_at(d), device_id_type=MESH)
        return carry

    def greet_head(d, carry):
        pl.semaphore_signal(
            barrier, inc=1, device_id=(c, lax.rem(h + d, HEADS)), device_id_type=MESH
        )
        return carry

    lax.fori_loop(1, CTX, greet_ctx, 0)
    lax.fori_loop(1, HEADS, greet_head, 0)

    own_rows = pl.ds(0, T)
    loads = [
        pltpu.make_async_copy(src, dst, in_sem.at[i])
        for i, (src, dst) in enumerate(
            (
                (b_hbm, b_ref),
                (c_hbm, c_ref),
                (x_hbm, x_ref),
                (ct_hbm, ct_ref),
                (k_hbm, kwin.at[own_rows]),
                (v_hbm, vwin.at[own_rows]),
                (q_hbm, q_ref),
                (do_hbm, do_ref),
            )
        )
    ]
    for load in loads:
        load.start()

    row_i = lax.broadcasted_iota(jnp.int32, (T, T), 0)
    col_i = lax.broadcasted_iota(jnp.int32, (T, T), 1)
    upto = (row_i <= col_i).astype(F32)
    low_half = col_i < 64

    cumr[...] = lax.dot_general(
        ld_ref[...], upto, NN, precision=lax.Precision.HIGHEST, preferred_element_type=F32
    )
    my_slab = pl.ds(pl.multiple_of(h * 16, 16), 16)

    pl.semaphore_wait(barrier, CTX - 1 + HEADS - 1)

    def doc_copy(d):
        return remote(doc_ref, docs.at[c], doc_ss.at[d], doc_rs.at[d], ctx_at(d))

    def doc_send(d, carry):
        doc_copy(d).start()
        return carry

    def slab_copies(d):
        device = (row_at(d), h)
        pairs = ((b_hbm, bg), (c_hbm, rg))
        return [
            remote(
                src.at[my_slab],
                dst.at[x, my_slab],
                bc_ss.at[d * 2 + i],
                bc_rs.at[d * 2 + i],
                device,
            )
            for i, (src, dst) in enumerate(pairs)
        ]

    def share_copies(d):
        device = (c, lax.rem(h + d, HEADS))
        return [
            remote(
                ref.at[:, my_slab, :],
                ref.at[:, my_slab, :],
                hd_ss.at[d * 2 + i],
                hd_rs.at[d * 2 + i],
                device,
            )
            for i, ref in enumerate((bg, rg))
        ]

    def decay_copy(d):
        t = lax.rem(x + d, NX)
        rows = cumr.at[pl.ds(pl.multiple_of(t * 8, 8), 8)]
        return remote(rows, dg.at[x], dc_ss.at[d], dc_rs.at[d], (y * NX + t, h))

    def token_copies(p, d):
        t = lax.rem(x + d, NX)
        src = lanes(t * 4 + p, T)
        dst = lanes(p, T)
        k = (p * NX + d) * 2
        return [
            remote(
                ref.at[:, src],
                out.at[x, :, dst],
                xa_ss.at[k + i],
                xa_rs.at[k + i],
                (y * NX + t, h),
            )
            for i, (ref, out) in enumerate(((x_hbm, xg), (ct_hbm, cg)))
        ]

    slabs = {d: slab_copies(d) for d in (1, 3, 2)}
    decays = {d: decay_copy(d) for d in (1, 3, 2)}
    for d in (1, 3, 2):
        for copy in slabs[d]:
            copy.start()
        decays[d].start()
    lax.fori_loop(1, CTX, doc_send, 0)

    def kv_copies(o):
        rows = pl.ds(pl.multiple_of(o * T, T), T)
        return (
            remote(k_hbm, kwin.at[rows], kv_ss.at[2 * o], kv_rs.at[2 * o], ctx_at(o)),
            remote(v_hbm, vwin.at[rows], kv_ss.at[2 * o + 1], kv_rs.at[2 * o + 1], ctx_at(o)),
        )

    def kv_send(o, carry):
        @pl.when(c + o < CTX)
        def _():
            for copy in kv_copies(o):
                copy.start()

        @pl.when(c < o)
        def _():
            rows = pl.ds(pl.multiple_of(o * T, T), T)
            kwin[rows, :] = jnp.zeros((T, T), BF16)
            vwin[rows, :] = jnp.zeros((T, T), BF16)

        return carry

    lax.fori_loop(1, WIN, kv_send, 0)

    def token_send(p, carry):
        for d in (1, 3, 2):
            for copy in token_copies(p, d):
                copy.start()
        return carry

    lax.fori_loop(0, 4, token_send, 0)

    for load in loads:
        load.wait()
    docs[c] = doc_ref[...]
    xg[x] = x_ref[:, lanes(x, GL)]
    cg[x] = ct_ref[:, lanes(x, GL)]
    bg[x, my_slab, :] = b_ref[my_slab, :]
    rg[x, my_slab, :] = c_ref[my_slab, :]
    dg[x] = cumr[pl.ds(pl.multiple_of(x * 8, 8), 8), :]

    for d in (1, 3, 2):
        for copy in slabs[d]:
            copy.wait_recv()

    def share(d, carry):
        for copy in share_copies(d):
            copy.start()
        return carry

    lax.fori_loop(1, HEADS, share, 0)

    doc_row = doc_ref[...].astype(F32)
    doc_col = column_of(doc_row)
    local_bias = jnp.where((doc_row == doc_col) & (col_i <= row_i), 0.0, NEG)
    gram = dot(c_ref[...], b_ref[...], NT)
    wsum[...] = jnp.zeros((T, T), F32)

    def columns(g, carry):
        rows = cumr[pl.ds(pl.multiple_of(g * 8, 8), 8), :]
        ccol[g] = jnp.concatenate([rows, jnp.zeros((T - 8, T), F32)], axis=0).T
        return carry

    lax.fori_loop(0, NG, columns, 0)
    half_mask = low_half.astype(BF16)
    other_mask = (~low_half).astype(BF16)

    def local_group(g, carry):
        rows = cumr[pl.ds(pl.multiple_of(g * 8, 8), 8), :]
        cols = ccol[g]
        total = wsum[...]
        for p in range(4):
            at = lanes(g * 4 + p, T)
            xp = x_ref[:, at]
            cp = ct_ref[:, at]
            x2 = jnp.concatenate([xp * half_mask, xp * other_mask], axis=0)
            c2 = jnp.concatenate([cp * half_mask, cp * other_mask], axis=0)
            inner = dot(c2, xp, NT)
            mix = []
            for i in range(2):
                j = 2 * p + i
                decay = jnp.exp(cols[:, j : j + 1] - rows[j : j + 1, :] + local_bias)
                mix.append((decay * gram).astype(BF16))
                total = total + decay * inner[i * T : (i + 1) * T]
            lo[:, at] = dot(jnp.concatenate(mix, axis=1), x2)
            lgx[:, at] = dot(jnp.concatenate(mix, axis=0), c2, TN)
        wsum[...] = total
        return carry

    lax.fori_loop(0, NG, local_group, 0)
    weighted = wsum[...].astype(BF16)
    gbl[:, 0:N] = dot(weighted, c_ref[...], TN)
    gbl[:, N : 2 * N] = dot(weighted, b_ref[...])

    def doc_wait(d, carry):
        doc_copy(d).wait_recv()
        return carry

    lax.fori_loop(1, CTX, doc_wait, 0)
    for d in (1, 3, 2):
        decays[d].wait_recv()

    def bias_block(o, carry):
        rows = pl.ds(pl.multiple_of(o * T, T), T)
        kb = lax.rem(c - o + CTX, CTX)
        key_doc = column_of(docs[kb].astype(F32))
        allowed = (key_doc == doc_row) & (kb * T + row_i <= c * T + col_i)
        block = jnp.where(allowed, 0.0, NEG)
        bias[rows, 0:T] = block
        bias[rows, T : 2 * T] = block
        return carry

    def stack_head(i, carry):
        rows = pl.ds(pl.multiple_of(i * T, T), T)
        qs[rows, :] = q_ref[:, lanes(i, T)]
        dos[rows, :] = do_ref[:, lanes(i, T)]
        return carry

    lax.fori_loop(0, WIN, bias_block, 0)
    lax.fori_loop(0, QL, stack_head, 0)

    def weights_of(j, carry):
        cum = dg[j]
        docj = docs[y * NX + j].astype(F32)
        start = jnp.where(docj == docj[:, 0:1], 1.0, 0.0)
        end = jnp.where(docj == docj[:, T - 1 : T], 1.0, 0.0)
        w_start = jnp.exp(cum) * start
        w_end = jnp.exp(cum[:, T - 1 : T] - cum) * end
        table = jnp.concatenate([w_start, w_end, jnp.zeros((T - 16, T), F32)], axis=0).T
        for p in range(4):
            at = slice(p * T, (p + 1) * T)
            ws = jnp.where(low_half, table[:, 2 * p : 2 * p + 1], table[:, 2 * p + 1 : 2 * p + 2])
            we = jnp.where(
                low_half, table[:, 8 + 2 * p : 9 + 2 * p], table[:, 9 + 2 * p : 10 + 2 * p]
            )
            wst[j, :, at] = ws
            wen[j, :, at] = we
            prow[j, :, at] = ws[T - 1 : T, :]
        return carry

    lax.fori_loop(0, NX, weights_of, 0)

    def edge(j, side):
        at = 0 if side == 0 else T - 1
        return docs[j].astype(F32)[:, at : at + 1]

    def linked(first, last, inside):
        same = edge(first, 0) == edge(last, 1)
        return jnp.where(same & inside, 1.0, 0.0)

    base = y * NX
    link = [linked(base, jnp.maximum(base - 1, 0), y > 0)]
    link += [linked(base + j, base + j - 1, y >= 0) for j in range(1, NX)]
    link += [linked(jnp.minimum(base + NX, CTX - 1), base + NX - 1, y < NX - 1)]
    wide = [jnp.broadcast_to(value, (1, GL)) for value in link]

    drow[0] = wide[0]
    for j in range(NX - 1):
        drow[j + 1] = wide[j + 1] * prow[j] * drow[j]
    drow[NX] = prow[NX - 1] * drow[NX - 1]
    erow[NX - 1] = wide[NX]
    for j in range(NX - 1, 0, -1):
        erow[j - 1] = wide[j] * prow[j] * erow[j]
    erow[NX] = prow[0] * erow[0]

    @pl.when(y == 0)
    def _():
        cin[...] = jnp.zeros((N, GL), BF16)

    @pl.when(y == NX - 1)
    def _():
        bin_[...] = jnp.zeros((N, GL), BF16)

    def kv_wait(o, carry):
        @pl.when(c >= o)
        def _():
            for copy in kv_copies(o):
                copy.wait_recv()

        return carry

    def turned_block(o, carry):
        rows = pl.ds(pl.multiple_of(o * T, T), T)
        kt[:, rows] = kwin[rows, :].T
        vt[:, rows] = vwin[rows, :].T
        return carry

    def head_pair(i, carry):
        two = 2 * T
        at = lanes(i, two)
        rows = pl.ds(pl.multiple_of(i * two, two), two)
        first = lanes(2 * i, T)
        second = lanes(2 * i + 1, T)
        q2 = qs[rows, :]
        do2 = dos[rows, :]
        scores = dot(kwin[...], q2, NT) * SCALE + bias[...]
        top = jnp.max(scores, axis=0, keepdims=True)
        weights = jnp.exp(scores - top)
        total = jnp.sum(weights, axis=0, keepdims=True)
        out_t = dot(vt[...], weights.astype(BF16)) / total
        out = out_t.T.astype(BF16)
        ao_ref[:, first] = out[:T]
        ao_ref[:, second] = out[T:]
        low = out_t.astype(BF16).astype(F32)
        inner = jnp.sum(low * do2.astype(F32).T, axis=0, keepdims=True)
        prob = weights * (1.0 / total)
        dscore = (prob * (dot(vwin[...], do2, NT) - inner)).astype(BF16)
        pall[:, at] = prob.astype(BF16)
        dsall[:, at] = dscore
        gq = (dot(kt[...], dscore) * SCALE).T.astype(BF16)
        gq_ref[:, first] = gq[:T]
        gq_ref[:, second] = gq[T:]
        return carry

    def row_grads(d):
        t = lax.rem(x + d, NX)
        device = (y * NX + t, h)
        blocks = (NX + x - t, lax.rem(2 * NX + x - t, 2 * NX))
        return [
            remote(
                dkv_s.at[o],
                dkv_r.at[2 * d + i],
                dkv_ss.at[2 * d + i],
                dkv_rs.at[2 * d + i],
                device,
            )
            for i, o in enumerate(blocks)
        ]

    def column_grads(r):
        device = (lax.rem(c + CTX - r * NX, CTX), h)
        return remote(up_s.at[r], up_r.at[r], up_ss.at[r], up_rs.at[r], device)

    def grads_block(o, carry):
        rows = pl.ds(pl.multiple_of(o * T, T), T)
        dkv_s[o, :, 0:T] = (dot(dsall[rows, :], qs[...]) * SCALE).astype(BF16)
        dkv_s[o, :, T : 2 * T] = dot(pall[rows, :], dos[...]).astype(BF16)
        return carry

    def share_wait(d, carry):
        for copy in share_copies(d):
            copy.wait_recv()
        return carry

    lax.fori_loop(1, HEADS, share_wait, 0)
    for j in range(NX):
        bt[j] = bg[j].T
        rt[j] = rg[j].T
        gc_acc[j] = jnp.zeros((T, N), F32)
        gb_acc[j] = jnp.zeros((T, N), F32)

    def block_sums(p):
        at = lanes(p, T)
        for d in (1, 3, 2):
            for copy in token_copies(p, d):
                copy.wait_recv()
        value = jnp.zeros((N, T), F32)
        for j in range(NX):
            term = (xg[j, :, at].astype(F32) * wen[j, :, at]).astype(BF16)
            xe[j, :, at] = term
            lst[j, :, at] = value
            value = prow[j, :, at] * value + dot(bt[j], term)
            if j < NX - 1:
                value = link[j + 1] * value
        lout[:, at] = value
        value = jnp.zeros((N, T), F32)
        for j in range(NX - 1, -1, -1):
            term = (cg[j, :, at].astype(F32) * wst[j, :, at]).astype(BF16)
            cs[j, :, at] = term
            rst[j, :, at] = value
            value = prow[j, :, at] * value + dot(rt[j], term)
            if j > 0:
                value = link[j] * value
        bout_l[:, at] = value

    def forward_copy(p):
        device = (lax.rem(c + NX, CTX), h)
        return remote(cout.at[p], cin.at[:, lanes(p, T)], cf_ss.at[p], cf_rs.at[p], device)

    def backward_copy(p):
        device = (lax.rem(c + CTX - NX, CTX), h)
        return remote(bout.at[p], bin_.at[:, lanes(p, T)], cb_ss.at[p], cb_rs.at[p], device)

    def forward_send(p):
        at = lanes(p, T)
        value = lout[:, at] + drow[NX, :, at] * cin[:, at].astype(F32)
        cout[p] = value.astype(BF16)
        forward_copy(p).start()

    def backward_send(p):
        at = lanes(p, T)
        value = bout_l[:, at] + erow[NX, :, at] * bin_[:, at].astype(F32)
        bout[p] = value.astype(BF16)
        backward_copy(p).start()

    def piece_copy(p, d, mine, theirs, send, recv):
        j = lax.rem(x + d, NX)
        k = p * NX + d
        return remote(mine.at[p, j], theirs.at[p, x], send.at[k], recv.at[k], (y * NX + j, h))

    def shared_copy(d, mine, theirs, k):
        e = lax.rem(h + d, HEADS)
        k = 2 * d + k
        return remote(mine.at[e], theirs.at[h], z_ss.at[k], z_rs.at[k], (c, e))

    def piece(p, local, scale, carried, proj, weight, terms, acc, mine, theirs, send, recv):
        at = lanes(p, T)
        value = carried[:, at].astype(F32)
        for d in (1, 3, 2, 0):
            j = lax.rem(x + d, NX)
            state = (local[j, :, at] + scale[j, :, at] * value).astype(BF16)
            out = (dot(proj[j], state) * weight[j, :, at]).astype(BF16)
            if d:
                mine[p, j] = out
                piece_copy(p, d, mine, theirs, send, recv).start()
            else:
                theirs[p, x] = out
            acc[j] += dot(terms[j, :, at], state, NT)

    def share_out(acc, first_lane, mine, theirs, k):
        acc[x] += gbl[:, first_lane : first_lane + N]
        for j in range(NX):
            mine[:, j, :, :] = acc[j].astype(BF16).reshape(HEADS, T // HEADS, N)

        def send(d, carry):
            shared_copy(d, mine, theirs, k).start()
            return carry

        lax.fori_loop(1, HEADS, send, 0)
        theirs[h] = mine[h]

    early = [
        pltpu.make_async_copy(ao_ref, ao_hbm, in_sem.at[0]),
        pltpu.make_async_copy(gq_ref, gq_hbm, in_sem.at[1]),
    ]

    def mixed(step, carry):
        pf = step - y
        pb = step - (NX - 1 - y)
        has_f = (pf >= 0) & (pf < 4)
        has_b = (pb >= 0) & (pb < 4)

        @pl.when(step < 4)
        def _():
            block_sums(step)

        @pl.when(has_f & (y > 0))
        def _():
            forward_copy(pf).wait_recv()

        @pl.when(has_f & (y < NX - 1))
        def _():
            forward_send(pf)

        @pl.when(has_b & (y < NX - 1))
        def _():
            backward_copy(pb).wait_recv()

        @pl.when(has_b & (y > 0))
        def _():
            backward_send(pb)

        @pl.when(has_f)
        def _():
            piece(pf, lst, drow, cin, rg, wst, cs, gc_acc, so_s, so_r, of_ss, of_rs)

        @pl.when(has_b)
        def _():
            piece(pb, rst, erow, bin_, bg, wen, xe, gb_acc, gx_s, gx_r, ob_ss, ob_rs)

        @pl.when(pf == 3)
        def _():
            share_out(gc_acc, N, gc_s, gc_r, 1)

        @pl.when(pb == 3)
        def _():
            share_out(gb_acc, 0, gb_s, gb_r, 0)

        @pl.when(step == 0)
        def _():
            lax.fori_loop(1, WIN, kv_wait, 0)
            lax.fori_loop(0, WIN, turned_block, 0)

        @pl.when(step < QL // 2)
        def _():
            head_pair(step, 0)

        @pl.when(step == 4)
        def _():
            for copy in early:
                copy.start()
            lax.fori_loop(1, 5, grads_block, 0)

        @pl.when(step == 5)
        def _():
            lax.fori_loop(5, WIN, grads_block, 0)
            for d in (1, 3, 2):
                first, second = row_grads(d)

                @pl.when(y > 0)
                def _():
                    first.start()

                @pl.when((lax.rem(x + d, NX) < x) | (y > 1))
                def _():
                    second.start()

        return carry

    lax.fori_loop(0, NX - 1 + 4, mixed, 0)

    own = slice(0, T)
    dkv_own[:, 0:T] = dot(dsall[own, :], qs[...]) * SCALE
    dkv_own[:, T : 2 * T] = dot(pall[own, :], dos[...])
    up_one[...] = dkv_s[NX].astype(F32)
    up_sum[...] = dkv_s[2 * NX].astype(F32)
    for d in (1, 3, 2):
        first, second = row_grads(d)

        @pl.when(y > 0)
        def _():
            first.wait_recv()
            up_one[...] += dkv_r[2 * d].astype(F32)

        @pl.when(x < d)
        def _():
            second.wait_recv()
            dkv_own[...] += dkv_r[2 * d + 1].astype(F32)

        @pl.when((x >= d) & (y > 1))
        def _():
            second.wait_recv()
            up_sum[...] += dkv_r[2 * d + 1].astype(F32)

    up_s[1] = up_one[...].astype(BF16)
    up_s[2] = up_sum[...].astype(BF16)
    for r in (1, 2):

        @pl.when(y >= r)
        def _():
            column_grads(r).start()

    def pieces_wait(p, carry):
        for d in (1, 3, 2):
            piece_copy(p, d, so_s, so_r, of_ss, of_rs).wait_recv()
            piece_copy(p, d, gx_s, gx_r, ob_ss, ob_rs).wait_recv()
        for s in range(NX):
            at = lanes(s * 4 + p, T)
            so_ref[:, at] = (lo[:, at] + so_r[p, s].astype(F32)).astype(BF16)
            gx_ref[:, at] = (lgx[:, at] + gx_r[p, s].astype(F32)).astype(BF16)
        return carry

    lax.fori_loop(0, 4, pieces_wait, 0)

    def shared_wait(d, carry):
        shared_copy(d, gb_s, gb_r, 0).wait_recv()
        shared_copy(d, gc_s, gc_r, 1).wait_recv()
        return carry

    lax.fori_loop(1, HEADS, shared_wait, 0)
    for k, ref in enumerate((gb_r, gc_r)):
        merged = ref[0].astype(F32)
        for e in range(1, HEADS):
            merged = merged + ref[e].astype(F32)
        gsum[:, k] = merged.astype(BF16)

    def owner_copy(d):
        j = lax.rem(x + d, NX)
        return remote(gsum.at[j], gr.at[x], gg_ss.at[d], gg_rs.at[d], (y * NX + j, h))

    for d in (1, 3, 2):
        owner_copy(d).start()
    gr[x] = gsum[x]

    for r in (1, 2):

        @pl.when(y + r < NX)
        def _():
            column_grads(r).wait_recv()
            dkv_own[...] += up_r[r].astype(F32)

    gk_ref[...] = dkv_own[:, 0:T].astype(BF16)
    gv_ref[...] = dkv_own[:, T : 2 * T].astype(BF16)

    for d in (1, 3, 2):
        owner_copy(d).wait_recv()
    owned = gr[0].astype(F32)
    for e in range(1, NX):
        owned = owned + gr[e].astype(F32)
    gb_ref[...] = owned[0].astype(BF16)
    gc_ref[...] = owned[1].astype(BF16)

    for r in (1, 2):

        @pl.when(y >= r)
        def _():
            column_grads(r).wait_send()

    for copy in early:
        copy.wait()

    def doc_done(d, carry):
        doc_copy(d).wait_send()
        return carry

    def kv_done(o, carry):
        @pl.when(c + o < CTX)
        def _():
            for copy in kv_copies(o):
                copy.wait_send()

        return carry

    def pieces_done(p, carry):
        for d in (1, 3, 2):
            for copy in token_copies(p, d):
                copy.wait_send()
            piece_copy(p, d, so_s, so_r, of_ss, of_rs).wait_send()
            piece_copy(p, d, gx_s, gx_r, ob_ss, ob_rs).wait_send()
        return carry

    def share_done(d, carry):
        for copy in share_copies(d):
            copy.wait_send()
        return carry

    def shared_done(d, carry):
        shared_copy(d, gb_s, gb_r, 0).wait_send()
        shared_copy(d, gc_s, gc_r, 1).wait_send()
        return carry

    def chain_done(p, carry):
        @pl.when(y < NX - 1)
        def _():
            forward_copy(p).wait_send()

        @pl.when(y > 0)
        def _():
            backward_copy(p).wait_send()

        return carry

    lax.fori_loop(1, CTX, doc_done, 0)
    lax.fori_loop(1, WIN, kv_done, 0)
    lax.fori_loop(0, 4, chain_done, 0)
    lax.fori_loop(0, 4, pieces_done, 0)
    lax.fori_loop(1, HEADS, share_done, 0)
    for d in (1, 3, 2):
        owner_copy(d).wait_send()
        decays[d].wait_send()
        for copy in slabs[d]:
            copy.wait_send()
        first, second = row_grads(d)

        @pl.when(y > 0)
        def _():
            first.wait_send()

        @pl.when((lax.rem(x + d, NX) < x) | (y > 1))
        def _():
            second.wait_send()

    lax.fori_loop(1, HEADS, shared_done, 0)


def body(q, k, v, do, doc, xs, b, cr, ld, ct):
    vm = pltpu.VMEM
    dma = pltpu.SemaphoreType.DMA
    scratch = [
        vm((T, QL * T), BF16),
        vm((T, QL * T), BF16),
        vm((T, QL * T), BF16),
        vm((T, QL * T), BF16),
        vm((T, NG * GL), BF16),
        vm((T, N), BF16),
        vm((T, N), BF16),
        vm((T, NG * GL), BF16),
        vm((KEYS, T), BF16),
        vm((KEYS, T), BF16),
        vm((T, KEYS), BF16),
        vm((T, KEYS), BF16),
        vm((CTX, 1, T), jnp.int32),
        vm((KEYS, 2 * T), F32),
        vm((QL * T, T), BF16),
        vm((QL * T, T), BF16),
        vm((KEYS, QL * T), BF16),
        vm((KEYS, QL * T), BF16),
        vm((T, 2 * T), F32),
        vm((WIN, T, 2 * T), BF16),
        vm((8, T, 2 * T), BF16),
        vm((T, 2 * T), F32),
        vm((T, 2 * T), F32),
        vm((3, T, 2 * T), BF16),
        vm((3, T, 2 * T), BF16),
        vm((NX, T, GL), BF16),
        vm((NX, T, GL), BF16),
        vm((NX, T, N), BF16),
        vm((NX, T, N), BF16),
        vm((32, T), F32),
        vm((NX, 8, T), F32),
        vm((NG, T, T), F32),
        vm((T, NG * GL), F32),
        vm((T, NG * GL), F32),
        vm((T, T), F32),
        vm((T, 2 * N), F32),
        vm((NX, T, GL), F32),
        vm((NX, T, GL), F32),
        vm((NX, T, GL), BF16),
        vm((NX, T, GL), BF16),
        vm((NX, N, T), BF16),
        vm((NX, N, T), BF16),
        vm((NX, N, GL), F32),
        vm((NX, N, GL), F32),
        vm((N, GL), F32),
        vm((N, GL), F32),
        vm((NX, 1, GL), F32),
        vm((NX + 1, 1, GL), F32),
        vm((NX + 1, 1, GL), F32),
        vm((N, GL), BF16),
        vm((4, N, T), BF16),
        vm((N, GL), BF16),
        vm((4, N, T), BF16),
        vm((4, NX, T, T), BF16),
        vm((4, NX, T, T), BF16),
        vm((4, NX, T, T), BF16),
        vm((4, NX, T, T), BF16),
        vm((NX, T, N), F32),
        vm((NX, T, N), F32),
        vm((HEADS, NX, T // HEADS, N), BF16),
        vm((HEADS, NX, T // HEADS, N), BF16),
        vm((HEADS, NX, T // HEADS, N), BF16),
        vm((HEADS, NX, T // HEADS, N), BF16),
        vm((NX, 2, T // HEADS, N), BF16),
        vm((NX, 2, T // HEADS, N), BF16),
        dma((8,)),
        dma((CTX,)),
        dma((CTX,)),
        dma((4,)),
        dma((4,)),
        dma((32,)),
        dma((32,)),
        dma((2 * WIN,)),
        dma((2 * WIN,)),
        dma((4,)),
        dma((4,)),
        dma((4,)),
        dma((4,)),
        dma((8,)),
        dma((8,)),
        dma((16,)),
        dma((16,)),
        dma((16,)),
        dma((16,)),
        dma((16,)),
        dma((16,)),
        dma((4,)),
        dma((4,)),
        dma((8,)),
        dma((8,)),
        dma((3,)),
        dma((3,)),
        dma((16,)),
        dma((16,)),
    ]
    shape = jax.ShapeDtypeStruct
    outs = (
        shape((T, QL * T), BF16),
        shape((T, NG * GL), BF16),
        shape((T, QL * T), BF16),
        shape((T, T), BF16),
        shape((T, T), BF16),
        shape((T, NG * GL), BF16),
        shape((T // HEADS, N), BF16),
        shape((T // HEADS, N), BF16),
    )
    here = pl.BlockSpec(memory_space=pltpu.VMEM)
    there = pl.BlockSpec(memory_space=pl.ANY)
    results = pl.pallas_call(
        kernel,
        name="packed_layers",
        out_shape=outs,
        in_specs=[there] * 4 + [here] + [there] * 3 + [here, there],
        out_specs=[there, here, there] + [here] * 5,
        scratch_shapes=scratch,
        compiler_params=pltpu.CompilerParams(
            collective_id=0, has_side_effects=True, vmem_limit_bytes=63 * 1024 * 1024
        ),
    )(q, k, v, do, doc.reshape(1, T), xs, b, cr, ld.T, ct)
    return pl.pallas_call(
        store,
        name="store_results",
        out_shape=outs,
        in_specs=[there] * 8,
        out_specs=[there] * 8,
        scratch_shapes=[pltpu.VMEM(out.shape, BF16) for out in outs] + [pltpu.SemaphoreType.DMA((16,))],
        compiler_params=pltpu.CompilerParams(vmem_limit_bytes=63 * 1024 * 1024),
    )(*results)


def store(*refs):
    sems = refs[24]
    copies = [
        (
            pltpu.make_async_copy(src, mid, sems.at[2 * i]),
            pltpu.make_async_copy(mid, dst, sems.at[2 * i + 1]),
        )
        for i, (src, dst, mid) in enumerate(zip(refs[:8], refs[8:16], refs[16:24]))
    ]
    for first, _ in copies:
        first.start()
    for first, second in copies:
        first.wait()
        second.start()
    for _, second in copies:
        second.wait()


def solution(mesh):
    both = P("ctx", "head")
    tokens = P("ctx", None)
    shared = P(("ctx", "head"), None)
    return jax.shard_map(
        body,
        mesh=mesh,
        in_specs=(both, both, both, both, P("ctx"), both, tokens, tokens, both, both),
        out_specs=(both, both, both, both, both, both, shared, shared),
        check_vma=False,
    )
```
